256 devices in a mesh: ray: 16 (over y, z_lo), pix: 16 (over z_hi, x, core).
Axes of the slice: x: 4, y: 4, z: 8 (z_hi: 2, z_lo: 4; z = z_hi * 4 + z_lo), core: 2. Of those that a mesh axis runs over, the one named last changes fastest.
Arguments:
- positions: float32 [2, 16384], P(None, 'ray'), may hold values from -2 to 2
- directions: float32 [2, 16384], P(None, 'ray'), may hold values from -0.35 to 0.35
- path: float32 [16384], P('ray'), may hold values from -9 to 9
- amplitude: float32 [16384], P('ray'), may hold values from 0.3 to 3
- psf_grad: float32 [3, 1024, 1024], P(None, 'pix', 'ray'), may hold values from -0.3 to 0.3
Outputs:
- psf: float32 [3, 1024, 1024], P(None, 'pix', 'ray')
- ray_grad: float32 [6, 16384], P(None, 'ray')
The draws below stay inside these ranges and needn't reach their ends.
All inputs are finite; a program needn't handle non-finite values.
Results may differ from the reference program's by a relative error of at most 0.0054.
Values may be sent and summed in bfloat16 or wider, within the bound.
A program may use at most 192 MiB of HBM per device.

```python
import math
import jax
import jax.numpy as jnp
from jax import lax

NPIX = 1024
NRAY = 16384


def levels(stream_key, shape, pieces, smallest, high):
    def one(dim, blocks):
        steps = jax.random.uniform(jax.random.fold_in(jax.random.fold_in(stream_key, 6), dim), (blocks,), jnp.float32, smallest / len(pieces), high / len(pieces))
        return jnp.repeat(jnp.exp(steps), shape[dim] // blocks).reshape((-1,) + (1,) * (len(shape) - dim - 1))

    loudness = one(*pieces[0])
    for cut in pieces[1:]:
        loudness = loudness * one(*cut)
    return loudness


def normal_values(key, extent, width, most, shards=(), kind=jnp.bfloat16):
    factor_of = levels(key, extent, shards, -0.22, 0.18) if shards else 1.0
    array = jax.random.normal(key, extent, jnp.float32) * width * factor_of
    return jnp.minimum(jnp.maximum(array, -most), most).astype(kind)


def setup_inputs(seed: int = 0) -> dict:
    key_of = jax.random.split(jax.random.key(seed), 6)
    positions = jnp.clip(jax.random.uniform(key_of[0], (2, NRAY), jnp.float32, -2.0, 2.0) * levels(key_of[0], (2, NRAY), ((1, 16),), -0.4, 0.0), -2.0, 2.0)
    directions = jnp.clip(jax.random.uniform(key_of[1], (2, NRAY), jnp.float32, -0.35, 0.35) * levels(key_of[1], (2, NRAY), ((1, 16),), -0.4, 0.0), -0.35, 0.35)
    path = normal_values(key_of[2], (NRAY,), 3.0, 9.0, ((0, 16),), jnp.float32)
    amplitude = jnp.clip(jnp.exp(math.log(3.0) - 2.3025851 * jax.random.uniform(key_of[3], (NRAY,), jnp.float32) ** levels(key_of[3], (NRAY,), ((0, 16),), -0.2, 0.2)), 0.3, 3.0)
    psf_grad = normal_values(key_of[4], (3, NPIX, NPIX), 0.05, 0.3, ((1, 16), (2, 16)), jnp.float32)
    return {"positions": positions, "directions": directions, "path": path, "amplitude": amplitude, "psf_grad": psf_grad}


wave_scales = (1.2088, 1.0, 0.8953)
two_pi = 2.0 * math.pi
highest = lax.Precision.HIGHEST

def centred(start, count):
    return (start + jnp.arange(count)).astype(jnp.float32) - 0.5 * NPIX + 0.5

def row_tables(block, rows_x, scale, norm):
    angle = scale * (block[4][:, None] + two_pi * (block[2][:, None] * (rows_x[None, :] - block[0][:, None]) - block[3][:, None] * block[1][:, None]))
    weight = (block[5] * norm)[:, None]
    return (weight * jnp.cos(angle), weight * jnp.sin(angle))

def col_tables(block, cols_y, scale):
    angle = scale * two_pi * cols_y[:, None] * block[3][None, :]
    return (jnp.cos(angle), jnp.sin(angle))

def mixing(a_re, a_im):
    upper = jnp.concatenate([a_re, a_im], axis=1)
    lower = jnp.concatenate([-a_im, a_re], axis=1)
    return jnp.concatenate([upper, lower], axis=0).astype(jnp.bfloat16)

def product(left, right, dims):
    return lax.dot_general(left.astype(jnp.float32), right.astype(jnp.float32), dims, precision=highest, preferred_element_type=jnp.float32)

def block_count(count):
    return max(1, min(16, count // 256))

def field_terms(rays, rows_x, cols_y, norm):
    count = rays.shape[1]
    nblk = block_count(count)
    blk = count // nblk

    def step(index, total):
        block = lax.dynamic_slice_in_dim(rays, (index * blk).astype(jnp.int32), blk, 1)
        parts = []
        for wave in range(3):
            scale = wave_scales[wave]
            a_re, a_im = row_tables(block, rows_x, scale, norm)
            b_re, b_im = col_tables(block, cols_y, scale)
            left = jnp.concatenate([b_re, b_im], axis=1).astype(jnp.bfloat16)
            parts.append(product(left, mixing(a_re, a_im), (((1,), (0,)), ((), ()))))
        return total + jnp.concatenate(parts, axis=1)
    init = jnp.zeros((cols_y.shape[0], 6 * rows_x.shape[0]), jnp.float32)
    return lax.fori_loop(0, nblk, step, init)

def ray_partials(rays, rows_x, cols_y, cotangent, norm):
    count = rays.shape[1]
    nblk = block_count(count)
    blk = count // nblk
    plen = rows_x.shape[0]

    def one_block(index):
        block = lax.dynamic_slice_in_dim(rays, (index * blk).astype(jnp.int32), blk, 1)
        first = jnp.zeros((blk,), jnp.float32)
        second = jnp.zeros((blk,), jnp.float32)
        third = jnp.zeros((blk,), jnp.float32)
        fourth = jnp.zeros((blk,), jnp.float32)
        for wave in range(3):
            scale = wave_scales[wave]
            a_re, a_im = row_tables(block, rows_x, scale, norm)
            b_re, b_im = col_tables(block, cols_y, scale)
            left = jnp.concatenate([b_re, b_im], axis=1).astype(jnp.bfloat16)
            mix = mixing(a_re, a_im)
            grad_u = cotangent[:, 2 * plen * wave:2 * plen * (wave + 1)]
            proj = product(left, grad_u, (((0,), (0,)), ((), ())))
            d_are = proj[:blk, :plen] + proj[blk:, plen:]
            d_aim = proj[:blk, plen:] - proj[blk:, :plen]
            d_b = product(grad_u, mix, (((1,), (1,)), ((), ())))
            d_beta = d_b[:, blk:] * b_re - d_b[:, :blk] * b_im
            d_alpha = d_aim * a_re - d_are * a_im
            first = first + scale * lax.optimization_barrier(jnp.sum(d_alpha, axis=1))
            second = second + scale * two_pi * lax.optimization_barrier(jnp.sum(d_alpha * rows_x[None, :], axis=1))
            third = third + scale * two_pi * lax.optimization_barrier(jnp.sum(d_beta * cols_y[:, None], axis=0))
            fourth = fourth + lax.optimization_barrier(jnp.sum(d_are * a_re + d_aim * a_im, axis=1))
        return jnp.stack([first, second, third, fourth])
    out = lax.map(one_block, jnp.arange(nblk))
    return jnp.transpose(out, (1, 0, 2)).reshape(4, count)

def finish(sums, rays):
    return jnp.stack([sums[0], -two_pi * rays[2] * sums[0], -two_pi * rays[3] * sums[0], (sums[1] - two_pi * rays[0] * sums[0]) / NPIX, (sums[2] - two_pi * rays[1] * sums[0]) / NPIX, sums[3] / rays[5]])

def reference(positions, directions, path, amplitude, psf_grad):
    rays = jnp.concatenate([positions, directions, path[None], amplitude[None]], axis=0)
    coords = centred(0, NPIX)
    norm = 1.0 / math.sqrt(NRAY)
    field = field_terms(rays, coords, coords, norm).reshape(NPIX, 3, 2, NPIX)
    psf = jnp.transpose(field[:, :, 0] ** 2 + field[:, :, 1] ** 2, (1, 2, 0))
    weight = jnp.transpose(psf_grad, (2, 0, 1))
    grad_u = (2.0 * weight[:, :, None, :] * field).reshape(NPIX, 6 * NPIX).astype(jnp.bfloat16)
    sums = ray_partials(rays, coords, coords, grad_u, norm)
    return (psf, finish(sums, rays))
```

```python
import functools
import math

import jax
import jax.numpy as jnp
from jax import lax
from jax.experimental import pallas as pl
from jax.experimental.pallas import tpu as pltpu
from jax.sharding import PartitionSpec as P

NPIX = 1024

wave_scales = (1.2088, 1.0, 0.8953)
two_pi = 2.0 * math.pi
MESH = pl.DeviceIdType.MESH

COS_COEF = (
    0.9999999890590201,
    -19.739204499453688,
    64.93911745988827,
    -85.45013953077586,
    60.16763095018129,
    -25.96759924584206,
    6.528658157862129,
)
SIN_COEF = (
    6.283185302511498,
    -41.341700405316736,
    81.60513138576982,
    -76.70301535347629,
    42.02592698341473,
    -14.899846660399582,
    3.2381375010236435,
)


def horner(coef, z):
    total = coef[-1] * z + coef[-2]
    for c in coef[-3::-1]:
        total = total * z + c
    return total


def cos_sin_turns(turns):
    frac = turns - jnp.round(turns)
    z = frac * frac
    return horner(COS_COEF, z), horner(SIN_COEF, z) * frac


def ladder(base, step_c, step_s, ntiles, store):
    c0, s0 = base
    cc, ss, cs, sc = c0 * step_c, s0 * step_s, c0 * step_s, s0 * step_c
    twice = step_c + step_c
    up = (cc - ss, sc + cs)
    down = (cc + ss, sc - cs)
    mid = ntiles // 2
    store(mid, base, up)
    back, last = base, up
    for k in range(mid + 2, ntiles, 2):
        first = (twice * last[0] - back[0], twice * last[1] - back[1])
        second = (twice * first[0] - last[0], twice * first[1] - last[1])
        store(k, first, second)
        back, last = first, second
    back, last = base, down
    nxt = (twice * last[0] - back[0], twice * last[1] - back[1])
    store(mid - 2, nxt, last)
    back, last = last, nxt
    for k in range(mid - 4, -1, -2):
        second = (twice * last[0] - back[0], twice * last[1] - back[1])
        first = (twice * second[0] - last[0], twice * second[1] - last[1])
        store(k, first, second)
        back, last = second, first


def kernel(
    n_ray,
    n_pix,
    pos_ref,
    dir_ref,
    path_ref,
    amp_ref,
    grad_ref,
    psf_ref,
    out_ref,
    pay,
    xt,
    yt,
    yf,
    acc,
    g2,
    v_loc,
    v_rem,
    lhs,
    s_snd,
    s_rcv,
    tot,
    fin,
    pay_send,
    pay_recv,
    g_sem,
    v_sem,
    s_send,
    s_recv,
    t_send,
    t_recv,
    f_sem,
):
    me = lax.axis_index("ray")
    pix = lax.axis_index("pix")
    core = lax.rem(pix, 2)
    pair = lax.div(pix, 2)
    n_pair = n_pix // 2
    partner = pix + 1 - 2 * core
    rows = NPIX // n_pair
    cols = NPIX // n_ray
    half = pay.shape[2]
    count = 2 * half
    norm = 1.0 / math.sqrt(count * n_ray)

    def ray_peer(k):
        return {"ray": lax.rem(me + k, n_ray)}

    def pair_peer(k):
        return {"pix": lax.rem(pix + 2 * k, n_pix)}

    barrier = pltpu.get_barrier_semaphore()

    def greet_ray(k, carry):
        pl.semaphore_signal(barrier, inc=1, device_id=ray_peer(k), device_id_type=MESH)
        return carry

    def greet_pair(k, carry):
        pl.semaphore_signal(barrier, inc=1, device_id=pair_peer(k), device_id_type=MESH)
        return carry

    lax.fori_loop(1, n_ray, greet_ray, 0)
    lax.fori_loop(1, n_pair, greet_pair, 0)
    pl.semaphore_signal(barrier, inc=1, device_id={"pix": partner}, device_id_type=MESH)

    mine = pl.ds(pl.multiple_of(core * half, 128), half)
    l_own = dir_ref[0:1, mine]
    m_own = dir_ref[1:2, mine]
    pay[me, 0:1, :] = (
        path_ref[0:1, mine] * (1.0 / two_pi) - l_own * pos_ref[0:1, mine] - m_own * pos_ref[1:2, mine]
    )
    pay[me, 1:2, :] = l_own
    pay[me, 2:3, :] = m_own
    pay[me, 3:4, :] = amp_ref[0:1, mine] * norm
    for wave in range(3):
        g = grad_ref[wave]
        g2[core, wave] = jnp.concatenate([g, g], axis=1)

    pl.semaphore_wait(barrier, n_ray + n_pair - 1)

    def pay_copy(k, slot):
        return pltpu.make_async_remote_copy(
            src_ref=pay.at[me],
            dst_ref=pay.at[slot],
            send_sem=pay_send.at[k],
            recv_sem=pay_recv.at[slot],
            device_id=ray_peer(n_ray - k),
            device_id_type=MESH,
        )

    def send_pay(k, carry):
        pay_copy(k, me).start()
        return carry

    lax.fori_loop(1, n_ray, send_pay, 0)

    def g_copy(slot):
        return pltpu.make_async_remote_copy(
            src_ref=g2.at[core],
            dst_ref=g2.at[slot],
            send_sem=g_sem.at[0],
            recv_sem=g_sem.at[1],
            device_id={"pix": partner},
            device_id_type=MESH,
        )

    g_copy(core).start()

    row_start = pair * rows
    col_start = me * cols
    sub = lax.broadcasted_iota(jnp.int32, (8, half), 0)
    x_base = (sub + (row_start + rows // 2)).astype(jnp.float32) - (0.5 * NPIX - 0.5)
    y_base = (sub + (col_start + cols // 2)).astype(jnp.float32) - (0.5 * NPIX - 0.5)
    wave_of = lax.rem(sub, 3)
    step_scale = 8.0 * jnp.where(
        wave_of == 0, wave_scales[0], jnp.where(wave_of == 1, wave_scales[1], wave_scales[2])
    )

    acc[...] = jnp.zeros_like(acc)

    def forward(block):
        rho = jnp.broadcast_to(pay[block, 0:1, :], (8, half))
        l_all = jnp.broadcast_to(pay[block, 1:2, :], (8, half))
        m_all = jnp.broadcast_to(pay[block, 2:3, :], (8, half))
        amp = jnp.broadcast_to(pay[block, 3:4, :], (8, half))
        step_c, step_s = cos_sin_turns(step_scale * jnp.where(sub < 3, l_all, m_all))
        x_turns = rho + l_all * x_base
        y_turns = m_all * y_base
        for wave in range(3):
            scale = wave_scales[wave]

            def store_x(k, first, second):
                for part in range(2):
                    tile = jnp.concatenate([first[part], second[part]], axis=0)
                    at = part * rows + 8 * k
                    xt[wave, block, at : at + 16, :] = tile.astype(jnp.bfloat16)

            def store_y(k, first, second):
                for part in range(2):
                    tile = jnp.concatenate([first[part], second[part]], axis=0)
                    at = part * cols + 8 * k
                    yf[wave, block, at : at + 16, :] = tile
                    yt[wave, block, at : at + 16, :] = tile.astype(jnp.bfloat16)

            def row_of(table, index):
                return jnp.broadcast_to(table[index : index + 1, :], (8, half))

            bc, bs = cos_sin_turns(scale * x_turns)
            ladder((amp * bc, amp * bs), row_of(step_c, wave), row_of(step_s, wave), rows // 8, store_x)
            ladder(
                cos_sin_turns(scale * y_turns),
                row_of(step_c, wave + 3),
                row_of(step_s, wave + 3),
                cols // 8,
                store_y,
            )
            acc[wave] += lax.dot_general(
                xt[wave, block],
                yt[wave, block],
                (((1,), (1,)), ((), ())),
                preferred_element_type=jnp.float32,
            )

    forward(me)

    def forward_step(k, carry):
        block = lax.rem(me + k, n_ray)
        pay_copy(k, block).wait_recv()
        forward(block)
        return carry

    lax.fori_loop(1, n_ray, forward_step, 0)

    low = lax.broadcasted_iota(jnp.int32, (rows, 2 * cols), 1) < cols
    for wave in range(3):
        other = acc[wave, rows : 2 * rows, :]
        v_loc[wave] = acc[wave, 0:rows, :] + pltpu.roll(jnp.where(low, other, -other), cols, 1)

    v_copy = pltpu.make_async_remote_copy(
        src_ref=v_loc,
        dst_ref=v_rem,
        send_sem=v_sem.at[0],
        recv_sem=v_sem.at[1],
        device_id={"pix": partner},
        device_id_type=MESH,
    )
    v_copy.start()
    g_copy(1 - core).wait_recv()
    v_copy.wait_recv()

    own_rows = pl.ds(pl.multiple_of(core * (rows // 2), 8), rows // 2)
    offset = (lax.broadcasted_iota(jnp.int32, (2 * cols // 2, rows), 1)).astype(jnp.float32) - (
        0.5 * rows - 0.5
    )
    for wave in range(3):
        own = v_loc[wave, own_rows, :] + v_rem[wave, own_rows, :]
        power = own * own
        psf_ref[wave] = (power + pltpu.roll(power, cols, 1))[:, :cols]
        field = v_loc[wave] + v_rem[wave]
        weight = jnp.concatenate([g2[0, wave], g2[1, wave]], axis=0)
        grad_t = jnp.transpose(2.0 * weight * field)
        re = grad_t[:cols]
        im = grad_t[cols:]
        lhs[wave, 0:cols, 0:rows] = re.astype(jnp.bfloat16)
        lhs[wave, 0:cols, rows:] = im.astype(jnp.bfloat16)
        lhs[wave, cols : 2 * cols, 0:rows] = im.astype(jnp.bfloat16)
        lhs[wave, cols : 2 * cols, rows:] = (-re).astype(jnp.bfloat16)
        re = re * offset
        im = im * offset
        lhs[wave, 2 * cols : 3 * cols, 0:rows] = re.astype(jnp.bfloat16)
        lhs[wave, 2 * cols : 3 * cols, rows:] = im.astype(jnp.bfloat16)
        lhs[wave, 3 * cols :, 0:rows] = im.astype(jnp.bfloat16)
        lhs[wave, 3 * cols :, rows:] = (-re).astype(jnp.bfloat16)

    x_mid = (row_start + rows // 2).astype(jnp.float32) - 0.5 * NPIX
    y_mid = (col_start + cols // 2).astype(jnp.float32) - 0.5 * NPIX

    def s_copy(block, slot):
        return pltpu.make_async_remote_copy(
            src_ref=s_snd.at[block],
            dst_ref=s_rcv.at[slot],
            send_sem=s_send.at[block],
            recv_sem=s_recv.at[slot],
            device_id={"ray": block},
            device_id_type=MESH,
        )

    def backward(block):
        s1 = jnp.zeros((8, half), jnp.float32)
        s2 = jnp.zeros((8, half), jnp.float32)
        s3 = jnp.zeros((8, half), jnp.float32)
        s4 = jnp.zeros((8, half), jnp.float32)
        sub_f = sub.astype(jnp.float32)
        for wave in range(3):
            d_b = lax.dot_general(
                lhs[wave],
                xt[wave, block],
                (((1,), (0,)), ((), ())),
                preferred_element_type=jnp.float32,
            )
            zi = jnp.zeros((8, half), jnp.float32)
            zx = jnp.zeros((8, half), jnp.float32)
            zy = jnp.zeros((8, half), jnp.float32)
            for t in range(cols // 8):
                at = 8 * t
                br = yf[wave, block, at : at + 8, :]
                bi = yf[wave, block, cols + at : cols + at + 8, :]
                dbr = d_b[at : at + 8]
                dbi = d_b[cols + at : cols + at + 8]
                dxr = d_b[2 * cols + at : 2 * cols + at + 8]
                dxi = d_b[3 * cols + at : 3 * cols + at + 8]
                d = br * dbi - bi * dbr
                zi = zi + d
                zy = zy + d * (sub_f + (at - 0.5 * cols + 0.5))
                zx = zx + (br * dxi - bi * dxr)
                s4 = s4 + (br * dbr + bi * dbi)
            scale = wave_scales[wave]
            s1 = s1 + scale * zi
            s2 = s2 + (scale * two_pi) * (x_mid * zi + zx)
            s3 = s3 + (scale * two_pi) * (y_mid * zi + zy)
        return [jnp.sum(s, axis=0, keepdims=True) for s in (s1, s2, s3, s4)]

    def backward_step(k, carry):
        block = lax.rem(me + k, n_ray)
        for i, s in enumerate(backward(block)):
            s_snd[block, i : i + 1, :] = s
        s_copy(block, me).start()
        return carry

    lax.fori_loop(1, n_ray, backward_step, 0)
    for i, s in enumerate(backward(me)):
        s_rcv[me, i : i + 1, :] = s

    def wait_s(k, carry):
        block = lax.rem(me + k, n_ray)
        s_copy(block, block).wait_recv()
        return carry

    lax.fori_loop(1, n_ray, wait_s, 0)
    total = s_rcv[0]
    for b in range(1, n_ray):
        total = total + s_rcv[b]
    tot[pair] = total

    def t_copy(k, slot):
        return pltpu.make_async_remote_copy(
            src_ref=tot.at[pair],
            dst_ref=tot.at[slot],
            send_sem=t_send.at[k],
            recv_sem=t_recv.at[slot],
            device_id=pair_peer(k),
            device_id_type=MESH,
        )

    def send_t(k, carry):
        t_copy(k, pair).start()
        return carry

    def wait_t(k, carry):
        t_copy(k, lax.rem(pair + k, n_pair)).wait_recv()
        return carry

    lax.fori_loop(1, n_pair, send_t, 0)
    lax.fori_loop(1, n_pair, wait_t, 0)
    total = tot[0]
    for b in range(1, n_pair):
        total = total + tot[b]
    fin[core] = total

    def f_copy(slot):
        return pltpu.make_async_remote_copy(
            src_ref=fin.at[core],
            dst_ref=fin.at[slot],
            send_sem=f_sem.at[0],
            recv_sem=f_sem.at[1],
            device_id={"pix": partner},
            device_id_type=MESH,
        )

    f_copy(core).start()
    f_copy(1 - core).wait_recv()

    for h in range(2):
        at = slice(h * half, (h + 1) * half)
        s1 = fin[h, 0:1, :]
        out_ref[0:1, at] = s1
        out_ref[1:2, at] = -two_pi * dir_ref[0:1, at] * s1
        out_ref[2:3, at] = -two_pi * dir_ref[1:2, at] * s1
        out_ref[3:4, at] = (fin[h, 1:2, :] - two_pi * pos_ref[0:1, at] * s1) * (1.0 / NPIX)
        out_ref[4:5, at] = (fin[h, 2:3, :] - two_pi * pos_ref[1:2, at] * s1) * (1.0 / NPIX)
        out_ref[5:6, at] = fin[h, 3:4, :] / amp_ref[0:1, at]

    def drain_ray(k, carry):
        pay_copy(k, me).wait_send()
        s_copy(lax.rem(me + k, n_ray), me).wait_send()
        return carry

    def drain_pair(k, carry):
        t_copy(k, pair).wait_send()
        return carry

    lax.fori_loop(1, n_ray, drain_ray, 0)
    lax.fori_loop(1, n_pair, drain_pair, 0)
    g_copy(core).wait_send()
    v_copy.wait_send()
    f_copy(core).wait_send()


def on_device(n_ray, n_pix, positions, directions, path, amplitude, psf_grad):
    count = positions.shape[1]
    half = count // 2
    n_pair = n_pix // 2
    rows = NPIX // n_pair
    cols = NPIX // n_ray
    f32 = jnp.float32
    bf16 = jnp.bfloat16
    vmem = pl.BlockSpec(memory_space=pltpu.VMEM)
    dma = pltpu.SemaphoreType.DMA
    return pl.pallas_call(
        functools.partial(kernel, n_ray, n_pix),
        out_shape=(
            jax.ShapeDtypeStruct(psf_grad.shape, f32),
            jax.ShapeDtypeStruct((6, count), f32),
        ),
        in_specs=[vmem] * 5,
        out_specs=(vmem, vmem),
        scratch_shapes=[
            pltpu.VMEM((n_ray, 4, half), f32),
            pltpu.VMEM((3, n_ray, 2 * rows, half), bf16),
            pltpu.VMEM((3, n_ray, 2 * cols, half), bf16),
            pltpu.VMEM((3, n_ray, 2 * cols, half), f32),
            pltpu.VMEM((3, 2 * rows, 2 * cols), f32),
            pltpu.VMEM((2, 3, rows // 2, 2 * cols), f32),
            pltpu.VMEM((3, rows, 2 * cols), f32),
            pltpu.VMEM((3, rows, 2 * cols), f32),
            pltpu.VMEM((3, 4 * cols, 2 * rows), bf16),
            pltpu.VMEM((n_ray, 4, half), f32),
            pltpu.VMEM((n_ray, 4, half), f32),
            pltpu.VMEM((n_pair, 4, half), f32),
            pltpu.VMEM((2, 4, half), f32),
            dma((n_ray,)),
            dma((n_ray,)),
            dma((2,)),
            dma((2,)),
            dma((n_ray,)),
            dma((n_ray,)),
            dma((n_pair,)),
            dma((n_pair,)),
            dma((2,)),
        ],
        compiler_params=pltpu.CompilerParams(
            collective_id=0, has_side_effects=True, vmem_limit_bytes=56 * 1024 * 1024
        ),
        name="ray_wave",
    )(positions, directions, path.reshape(1, count), amplitude.reshape(1, count), psf_grad)


def solution(mesh):
    in_specs = (P(None, "ray"), P(None, "ray"), P("ray"), P("ray"), P(None, "pix", "ray"))
    out_specs = (P(None, "pix", "ray"), P(None, "ray"))
    body = functools.partial(on_device, mesh.shape["ray"], mesh.shape["pix"])
    return jax.shard_map(
        body, mesh=mesh, in_specs=in_specs, out_specs=out_specs, check_vma=False
    )
```

```python
import functools
import math

import jax
import jax.numpy as jnp
from jax import lax
from jax.experimental import pallas as pl
from jax.experimental.pallas import tpu as pltpu
from jax.sharding import PartitionSpec as P

NPIX = 1024

wave_scales = (1.2088, 1.0, 0.8953)
two_pi = 2.0 * math.pi
MESH = pl.DeviceIdType.MESH

COS_COEF = (
    0.9999999890590201,
    -19.739204499453688,
    64.93911745988827,
    -85.45013953077586,
    60.16763095018129,
    -25.96759924584206,
    6.528658157862129,
)
SIN_COEF = (
    6.283185302511498,
    -41.341700405316736,
    81.60513138576982,
    -76.70301535347629,
    42.02592698341473,
    -14.899846660399582,
    3.2381375010236435,
)


def horner(coef, z):
    total = coef[-1] * z + coef[-2]
    for c in coef[-3::-1]:
        total = total * z + c
    return total


def cos_sin_turns(turns):
    frac = turns - jnp.round(turns)
    z = frac * frac
    return horner(COS_COEF, z), horner(SIN_COEF, z) * frac


def ladder(base, step_c, step_s, ntiles, store):
    c0, s0 = base
    cc, ss, cs, sc = c0 * step_c, s0 * step_s, c0 * step_s, s0 * step_c
    twice = step_c + step_c
    up = (cc - ss, sc + cs)
    down = (cc + ss, sc - cs)
    mid = ntiles // 2
    store(mid, base, up)
    back, last = base, up
    for k in range(mid + 2, ntiles, 2):
        first = (twice * last[0] - back[0], twice * last[1] - back[1])
        second = (twice * first[0] - last[0], twice * first[1] - last[1])
        store(k, first, second)
        back, last = first, second
    back, last = base, down
    nxt = (twice * last[0] - back[0], twice * last[1] - back[1])
    store(mid - 2, nxt, last)
    back, last = last, nxt
    for k in range(mid - 4, -1, -2):
        second = (twice * last[0] - back[0], twice * last[1] - back[1])
        first = (twice * second[0] - last[0], twice * second[1] - last[1])
        store(k, first, second)
        back, last = second, first


def offset_of(k):
    b, a = k >> 2, k & 3
    b3, a3 = (b >> 1) * (b & 1), (a >> 1) * (a & 1)
    dy = b + (b >> 1) - 2 * b3
    dz = a + 5 * (a >> 1) - 6 * a3 + 4 * a3 * (dy & 1)
    return dy, dz


def kernel(
    n_ray,
    n_pix,
    pos_hbm,
    dir_hbm,
    path_hbm,
    amp_hbm,
    grad_hbm,
    psf_hbm,
    out_hbm,
    pos_ref,
    dir_ref,
    path_ref,
    amp_ref,
    grad_ref,
    psf_ref,
    out_ref,
    pay,
    xt,
    yt,
    yf,
    acc,
    g2,
    v_loc,
    v_rem,
    lhs,
    s_snd,
    s_rcv,
    tot,
    in_sem,
    out_sem,
    pay_send,
    pay_recv,
    g_sem,
    v_sem,
    s_send,
    s_recv,
    t_send,
    t_recv,
):
    me = lax.axis_index("ray")
    pix = lax.axis_index("pix")
    core = pix & 1
    pair = pix >> 1
    x_pos = pair & 3
    y_pos = me >> 2
    z_pos = 4 * (pair >> 2) + (me & 3)
    n_pair = n_pix // 2
    partner = pix + 1 - 2 * core
    rows = NPIX // n_pair
    cols = NPIX // n_ray
    half = pay.shape[2]
    count = 2 * half
    norm = 1.0 / math.sqrt(count * n_ray)

    def chip_at(dy, dz):
        y = (y_pos + dy) & 3
        z = (z_pos + dz) & 7
        return {"ray": 4 * y + (z & 3), "pix": 8 * (z >> 2) + (pix & 7)}

    def block_of(k):
        dy, dz = offset_of(k)
        return 4 * ((y_pos + dy) & 3) + ((z_pos + dz) & 3)

    loads = [
        pltpu.make_async_copy(src, dst, in_sem.at[i])
        for i, (src, dst) in enumerate(
            (
                (pos_hbm, pos_ref),
                (dir_hbm, dir_ref),
                (path_hbm, path_ref),
                (amp_hbm, amp_ref),
                (grad_hbm, grad_ref),
            )
        )
    ]
    for load in loads:
        load.start()

    def wait_bytes(ref, sem):
        pltpu.make_async_copy(ref, ref, sem).wait()

    barrier = pltpu.get_barrier_semaphore()

    def x_peer(dx, other):
        return {"pix": (pix & 8) + 2 * ((x_pos + dx) & 3) + (core + other - 2 * core * other)}

    x_others = [(dx, other) for dx in range(4) for other in range(2)][1:]

    for dy, dz in [(dy, dz) for dy in range(4) for dz in (0, 1, 7, 2, 6)][1:]:
        pl.semaphore_signal(barrier, inc=1, device_id=chip_at(dy, dz), device_id_type=MESH)
    for dx, other in x_others:
        pl.semaphore_signal(barrier, inc=1, device_id=x_peer(dx, other), device_id_type=MESH)

    for load in loads[:4]:
        load.wait()
    mine = pl.ds(pl.multiple_of(core * half, 128), half)
    l_own = dir_ref[0:1, mine]
    m_own = dir_ref[1:2, mine]
    pay[me, 0:1, :] = (
        path_ref[0:1, mine] * (1.0 / two_pi) - l_own * pos_ref[0:1, mine] - m_own * pos_ref[1:2, mine]
    )
    pay[me, 1:2, :] = l_own
    pay[me, 2:3, :] = m_own
    pay[me, 3:4, :] = amp_ref[0:1, mine] * norm

    pl.semaphore_wait(barrier, 26)

    def pay_copy(k, slot):
        dy, dz = offset_of(k)
        return pltpu.make_async_remote_copy(
            src_ref=pay.at[me],
            dst_ref=pay.at[slot],
            send_sem=pay_send.at[0],
            recv_sem=pay_recv.at[slot],
            device_id=chip_at(4 - dy, 8 - dz),
            device_id_type=MESH,
        )

    for k in range(1, n_ray):
        pay_copy(k, me).start()

    loads[4].wait()
    for wave in range(3):
        g = grad_ref[wave]
        g2[core, wave] = jnp.concatenate([g, g], axis=1)

    def g_copy(slot):
        return pltpu.make_async_remote_copy(
            src_ref=g2.at[core],
            dst_ref=g2.at[slot],
            send_sem=g_sem.at[0],
            recv_sem=g_sem.at[1],
            device_id={"pix": partner},
            device_id_type=MESH,
        )

    g_copy(core).start()

    row_start = pair * rows
    col_start = me * cols
    sub = lax.broadcasted_iota(jnp.int32, (8, half), 0)
    x_base = (sub + (row_start + rows // 2)).astype(jnp.float32) - (0.5 * NPIX - 0.5)
    y_base = (sub + (col_start + cols // 2)).astype(jnp.float32) - (0.5 * NPIX - 0.5)
    wave_of = lax.rem(sub, 3)
    step_scale = 8.0 * jnp.where(
        wave_of == 0, wave_scales[0], jnp.where(wave_of == 1, wave_scales[1], wave_scales[2])
    )

    acc[...] = jnp.zeros_like(acc)

    def forward(block):
        rho = jnp.broadcast_to(pay[block, 0:1, :], (8, half))
        l_all = jnp.broadcast_to(pay[block, 1:2, :], (8, half))
        m_all = jnp.broadcast_to(pay[block, 2:3, :], (8, half))
        amp = jnp.broadcast_to(pay[block, 3:4, :], (8, half))
        step_c, step_s = cos_sin_turns(step_scale * jnp.where(sub < 3, l_all, m_all))
        x_turns = rho + l_all * x_base
        y_turns = m_all * y_base
        for wave in range(3):
            scale = wave_scales[wave]

            def store_x(k, first, second):
                for part in range(2):
                    tile = jnp.concatenate([first[part], second[part]], axis=0)
                    at = part * rows + 8 * k
                    xt[wave, block, at : at + 16, :] = tile.astype(jnp.bfloat16)

            def store_y(k, first, second):
                for part in range(2):
                    tile = jnp.concatenate([first[part], second[part]], axis=0)
                    at = part * cols + 8 * k
                    yf[wave, block, at : at + 16, :] = tile
                    yt[wave, block, at : at + 16, :] = tile.astype(jnp.bfloat16)

            def row_of(table, index):
                return jnp.broadcast_to(table[index : index + 1, :], (8, half))

            bc, bs = cos_sin_turns(scale * x_turns)
            ladder((amp * bc, amp * bs), row_of(step_c, wave), row_of(step_s, wave), rows // 8, store_x)
            ladder(
                cos_sin_turns(scale * y_turns),
                row_of(step_c, wave + 3),
                row_of(step_s, wave + 3),
                cols // 8,
                store_y,
            )
            acc[wave] += lax.dot_general(
                xt[wave, block],
                yt[wave, block],
                (((1,), (1,)), ((), ())),
                preferred_element_type=jnp.float32,
            )

    forward(me)

    def forward_step(k, carry):
        block = block_of(k)
        pay_copy(k, block).wait_recv()
        forward(block)
        return carry

    lax.fori_loop(1, n_ray, forward_step, 0)

    low = lax.broadcasted_iota(jnp.int32, (rows, 2 * cols), 1) < cols
    for wave in range(3):
        other = acc[wave, rows : 2 * rows, :]
        v_loc[wave] = acc[wave, 0:rows, :] + pltpu.roll(jnp.where(low, other, -other), cols, 1)

    v_copy = pltpu.make_async_remote_copy(
        src_ref=v_loc,
        dst_ref=v_rem,
        send_sem=v_sem.at[0],
        recv_sem=v_sem.at[1],
        device_id={"pix": partner},
        device_id_type=MESH,
    )
    v_copy.start()
    g_copy(1 - core).wait_recv()
    v_copy.wait_recv()

    own_rows = pl.ds(pl.multiple_of(core * (rows // 2), 8), rows // 2)
    offset = (lax.broadcasted_iota(jnp.int32, (2 * cols // 2, rows), 1)).astype(jnp.float32) - (
        0.5 * rows - 0.5
    )
    for wave in range(3):
        own = v_loc[wave, own_rows, :] + v_rem[wave, own_rows, :]
        power = own * own
        psf_ref[wave] = (power + pltpu.roll(power, cols, 1))[:, :cols]
        field = v_loc[wave] + v_rem[wave]
        weight = jnp.concatenate([g2[0, wave], g2[1, wave]], axis=0)
        grad_t = jnp.transpose(2.0 * weight * field)
        re = grad_t[:cols]
        im = grad_t[cols:]
        lhs[wave, 0:cols, 0:rows] = re.astype(jnp.bfloat16)
        lhs[wave, 0:cols, rows:] = im.astype(jnp.bfloat16)
        lhs[wave, cols : 2 * cols, 0:rows] = im.astype(jnp.bfloat16)
        lhs[wave, cols : 2 * cols, rows:] = (-re).astype(jnp.bfloat16)
        re = re * offset
        im = im * offset
        lhs[wave, 2 * cols : 3 * cols, 0:rows] = re.astype(jnp.bfloat16)
        lhs[wave, 2 * cols : 3 * cols, rows:] = im.astype(jnp.bfloat16)
        lhs[wave, 3 * cols :, 0:rows] = im.astype(jnp.bfloat16)
        lhs[wave, 3 * cols :, rows:] = (-re).astype(jnp.bfloat16)

    psf_store = pltpu.make_async_copy(psf_ref, psf_hbm, out_sem.at[0])
    psf_store.start()

    x_mid = (row_start + rows // 2).astype(jnp.float32) - 0.5 * NPIX
    y_mid = (col_start + cols // 2).astype(jnp.float32) - 0.5 * NPIX

    here = 8 * y_pos + z_pos

    def s_copy(k, far):
        dy, dz = offset_of(k)
        return pltpu.make_async_remote_copy(
            src_ref=s_snd.at[k],
            dst_ref=s_rcv.at[here],
            send_sem=s_send.at[0],
            recv_sem=s_recv.at[0],
            device_id=chip_at(dy, dz + 4 * far),
            device_id_type=MESH,
        )

    def backward(block):
        s1 = jnp.zeros((8, half), jnp.float32)
        s2 = jnp.zeros((8, half), jnp.float32)
        s3 = jnp.zeros((8, half), jnp.float32)
        s4 = jnp.zeros((8, half), jnp.float32)
        sub_f = sub.astype(jnp.float32)
        for wave in range(3):
            d_b = lax.dot_general(
                lhs[wave],
                xt[wave, block],
                (((1,), (0,)), ((), ())),
                preferred_element_type=jnp.float32,
            )
            zi = jnp.zeros((8, half), jnp.float32)
            zx = jnp.zeros((8, half), jnp.float32)
            zy = jnp.zeros((8, half), jnp.float32)
            for t in range(cols // 8):
                at = 8 * t
                br = yf[wave, block, at : at + 8, :]
                bi = yf[wave, block, cols + at : cols + at + 8, :]
                dbr = d_b[at : at + 8]
                dbi = d_b[cols + at : cols + at + 8]
                dxr = d_b[2 * cols + at : 2 * cols + at + 8]
                dxi = d_b[3 * cols + at : 3 * cols + at + 8]
                d = br * dbi - bi * dbr
                zi = zi + d
                zy = zy + d * (sub_f + (at - 0.5 * cols + 0.5))
                zx = zx + (br * dxi - bi * dxr)
                s4 = s4 + (br * dbr + bi * dbi)
            scale = wave_scales[wave]
            s1 = s1 + scale * zi
            s2 = s2 + (scale * two_pi) * (x_mid * zi + zx)
            s3 = s3 + (scale * two_pi) * (y_mid * zi + zy)
        sums = [jnp.sum(s, axis=0, keepdims=True) for s in (s1, s2, s3, s4)]
        return jnp.concatenate(
            [s[:, 128 * t : 128 * t + 128] for s in sums for t in range(half // 128)], axis=0
        )

    def backward_step(i, carry):
        k = n_ray - i
        s_snd[k] = backward(block_of(k)).astype(jnp.bfloat16)
        s_copy(k, 1).start()
        s_copy(k, 0).start()
        return carry

    lax.fori_loop(1, n_ray, backward_step, 0)
    s_own = backward(me).astype(jnp.bfloat16)
    s_snd[0] = s_own
    s_copy(0, 1).start()
    s_rcv[here] = s_own
    wait_bytes(s_rcv.at[0:31], s_recv.at[0])
    total = s_rcv[0].astype(jnp.float32)
    for b in range(1, 32):
        total = total + s_rcv[b].astype(jnp.float32)
    tot[4 * core + x_pos] = total

    for dx, other in x_others:
        pltpu.make_async_remote_copy(
            src_ref=tot.at[4 * core + x_pos],
            dst_ref=tot.at[4 * core + x_pos],
            send_sem=t_send.at[0],
            recv_sem=t_recv.at[0],
            device_id=x_peer(dx, other),
            device_id_type=MESH,
        ).start()
    wait_bytes(tot.at[0:7], t_recv.at[0])
    tiles = half // 128
    for h in range(2):
        total = tot[4 * h]
        for b in range(1, 4):
            total = total + tot[4 * h + b]
        for t in range(tiles):
            at = slice(h * half + 128 * t, h * half + 128 * t + 128)
            s1, s2, s3, s4 = (total[tiles * i + t : tiles * i + t + 1] for i in range(4))
            out_ref[0:1, at] = s1
            out_ref[1:2, at] = -two_pi * dir_ref[0:1, at] * s1
            out_ref[2:3, at] = -two_pi * dir_ref[1:2, at] * s1
            out_ref[3:4, at] = (s2 - two_pi * pos_ref[0:1, at] * s1) * (1.0 / NPIX)
            out_ref[4:5, at] = (s3 - two_pi * pos_ref[1:2, at] * s1) * (1.0 / NPIX)
            out_ref[5:6, at] = s4 / amp_ref[0:1, at]
    out_store = pltpu.make_async_copy(out_ref, out_hbm, out_sem.at[1])
    out_store.start()

    wait_bytes(pay.at[0 : n_ray - 1], pay_send.at[0])
    wait_bytes(s_rcv.at[0:31], s_send.at[0])
    wait_bytes(tot.at[0:7], t_send.at[0])
    g_copy(core).wait_send()
    v_copy.wait_send()
    psf_store.wait()
    out_store.wait()


def on_device(n_ray, n_pix, positions, directions, path, amplitude, psf_grad):
    count = positions.shape[1]
    half = count // 2
    n_pair = n_pix // 2
    rows = NPIX // n_pair
    cols = NPIX // n_ray
    f32 = jnp.float32
    bf16 = jnp.bfloat16
    any_space = pl.BlockSpec(memory_space=pl.ANY)
    dma = pltpu.SemaphoreType.DMA
    return pl.pallas_call(
        functools.partial(kernel, n_ray, n_pix),
        out_shape=(
            jax.ShapeDtypeStruct(psf_grad.shape, f32),
            jax.ShapeDtypeStruct((6, count), f32),
        ),
        in_specs=[any_space] * 5,
        out_specs=(any_space, any_space),
        scratch_shapes=[
            pltpu.VMEM((2, count), f32),
            pltpu.VMEM((2, count), f32),
            pltpu.VMEM((1, count), f32),
            pltpu.VMEM((1, count), f32),
            pltpu.VMEM(psf_grad.shape, f32),
            pltpu.VMEM(psf_grad.shape, f32),
            pltpu.VMEM((6, count), f32),
            pltpu.VMEM((n_ray, 4, half), f32),
            pltpu.VMEM((3, n_ray, 2 * rows, half), bf16),
            pltpu.VMEM((3, n_ray, 2 * cols, half), bf16),
            pltpu.VMEM((3, n_ray, 2 * cols, half), f32),
            pltpu.VMEM((3, 2 * rows, 2 * cols), f32),
            pltpu.VMEM((2, 3, rows // 2, 2 * cols), f32),
            pltpu.VMEM((3, rows, 2 * cols), f32),
            pltpu.VMEM((3, rows, 2 * cols), f32),
            pltpu.VMEM((3, 4 * cols, 2 * rows), bf16),
            pltpu.VMEM((n_ray, half // 32, 128), bf16),
            pltpu.VMEM((32, half // 32, 128), bf16),
            pltpu.VMEM((8, half // 32, 128), f32),
            dma((5,)),
            dma((2,)),
            dma((1,)),
            dma((n_ray,)),
            dma((2,)),
            dma((2,)),
            dma((1,)),
            dma((1,)),
            dma((1,)),
            dma((1,)),
        ],
        compiler_params=pltpu.CompilerParams(
            collective_id=0, has_side_effects=True, vmem_limit_bytes=56 * 1024 * 1024
        ),
        name="ray_wave",
    )(positions, directions, path.reshape(1, count), amplitude.reshape(1, count), psf_grad)


def solution(mesh):
    in_specs = (P(None, "ray"), P(None, "ray"), P("ray"), P("ray"), P(None, "pix", "ray"))
    out_specs = (P(None, "pix", "ray"), P(None, "ray"))
    body = functools.partial(on_device, mesh.shape["ray"], mesh.shape["pix"])
    return jax.shard_map(
        body, mesh=mesh, in_specs=in_specs, out_specs=out_specs, check_vma=False
    )
```

```python
import functools
import math

import jax
import jax.numpy as jnp
from jax import lax
from jax.experimental import pallas as pl
from jax.experimental.pallas import tpu as pltpu
from jax.sharding import PartitionSpec as P

NPIX = 1024

wave_scales = (1.2088, 1.0, 0.8953)
two_pi = 2.0 * math.pi
MESH = pl.DeviceIdType.MESH

COS_COEF = (
    0.9999999890590201,
    -19.739204499453688,
    64.93911745988827,
    -85.45013953077586,
    60.16763095018129,
    -25.96759924584206,
    6.528658157862129,
)
SIN_COEF = (
    6.283185302511498,
    -41.341700405316736,
    81.60513138576982,
    -76.70301535347629,
    42.02592698341473,
    -14.899846660399582,
    3.2381375010236435,
)


def horner(coef, z):
    total = coef[-1] * z + coef[-2]
    for c in coef[-3::-1]:
        total = total * z + c
    return total


def cos_sin_turns(turns):
    frac = turns - jnp.round(turns)
    z = frac * frac
    return horner(COS_COEF, z), horner(SIN_COEF, z) * frac


def ladder(base, step_c, step_s, ntiles, store):
    c0, s0 = base
    cc, ss, cs, sc = c0 * step_c, s0 * step_s, c0 * step_s, s0 * step_c
    twice = step_c + step_c
    up = (cc - ss, sc + cs)
    down = (cc + ss, sc - cs)
    mid = ntiles // 2
    store(mid, base, up)
    back, last = base, up
    for k in range(mid + 2, ntiles, 2):
        first = (twice * last[0] - back[0], twice * last[1] - back[1])
        second = (twice * first[0] - last[0], twice * first[1] - last[1])
        store(k, first, second)
        back, last = first, second
    back, last = base, down
    nxt = (twice * last[0] - back[0], twice * last[1] - back[1])
    store(mid - 2, nxt, last)
    back, last = last, nxt
    for k in range(mid - 4, -1, -2):
        second = (twice * last[0] - back[0], twice * last[1] - back[1])
        first = (twice * second[0] - last[0], twice * second[1] - last[1])
        store(k, first, second)
        back, last = second, first


def offset_of(k):
    b, a = k >> 2, k & 3
    b3, a3 = (b >> 1) * (b & 1), (a >> 1) * (a & 1)
    dy = b + (b >> 1) - 2 * b3
    dz = a + 5 * (a >> 1) - 6 * a3 + 4 * a3 * (dy & 1)
    return dy, dz


def kernel(
    n_ray,
    n_pix,
    pos_hbm,
    dir_hbm,
    path_hbm,
    amp_hbm,
    grad_hbm,
    psf_hbm,
    out_hbm,
    pos_ref,
    dir_ref,
    path_ref,
    amp_ref,
    grad_ref,
    psf_ref,
    out_ref,
    pay,
    xt0,
    xt1,
    xt2,
    yt0,
    yt1,
    yt2,
    yf0,
    yf1,
    yf2,
    v_loc0,
    v_loc1,
    v_loc2,
    g2,
    v_rem,
    power,
    lhs,
    s_snd,
    s_rcv,
    tot,
    in_sem,
    out_sem,
    pay_send,
    pay_recv,
    g_sem,
    v_sem,
    s_send,
    s_recv,
    t_send,
    t_recv,
):
    me = lax.axis_index("ray")
    pix = lax.axis_index("pix")
    xt, yt, yf, v_loc = (xt0, xt1, xt2), (yt0, yt1, yt2), (yf0, yf1, yf2), (v_loc0, v_loc1, v_loc2)
    core = pix & 1
    pair = pix >> 1
    x_pos = pair & 3
    y_pos = me >> 2
    z_pos = 4 * (pair >> 2) + (me & 3)
    n_pair = n_pix // 2
    partner = pix + 1 - 2 * core
    rows = NPIX // n_pair
    cols = NPIX // n_ray
    half = pay.shape[2]
    count = 2 * half
    norm = 1.0 / math.sqrt(count * n_ray)

    def chip_at(dy, dz):
        y = (y_pos + dy) & 3
        z = (z_pos + dz) & 7
        return {"ray": 4 * y + (z & 3), "pix": 8 * (z >> 2) + (pix & 7)}

    def block_of(k):
        dy, dz = offset_of(k)
        return 4 * ((y_pos + dy) & 3) + ((z_pos + dz) & 3)

    loads = [
        pltpu.make_async_copy(src, dst, in_sem.at[i])
        for i, (src, dst) in enumerate(
            (
                (pos_hbm, pos_ref),
                (dir_hbm, dir_ref),
                (path_hbm, path_ref),
                (amp_hbm, amp_ref),
                (grad_hbm, grad_ref),
            )
        )
    ]
    for load in loads:
        load.start()

    def wait_bytes(ref, sem):
        pltpu.make_async_copy(ref, ref, sem).wait()

    barrier = pltpu.get_barrier_semaphore()

    def x_peer(dx, other):
        return {"pix": (pix & 8) + 2 * ((x_pos + dx) & 3) + (core + other - 2 * core * other)}

    x_others = [(dx, other) for dx in range(4) for other in range(2)][1:]

    for dy, dz in [(dy, dz) for dy in range(4) for dz in (0, 1, 7, 2, 6)][1:]:
        pl.semaphore_signal(barrier, inc=1, device_id=chip_at(dy, dz), device_id_type=MESH)
    for dx, other in x_others:
        pl.semaphore_signal(barrier, inc=1, device_id=x_peer(dx, other), device_id_type=MESH)

    for load in loads[:4]:
        load.wait()
    mine = pl.ds(pl.multiple_of(core * half, 128), half)
    l_own = dir_ref[0:1, mine]
    m_own = dir_ref[1:2, mine]
    pay[me, 0:1, :] = (
        path_ref[0:1, mine] * (1.0 / two_pi) - l_own * pos_ref[0:1, mine] - m_own * pos_ref[1:2, mine]
    )
    pay[me, 1:2, :] = l_own
    pay[me, 2:3, :] = m_own
    pay[me, 3:4, :] = amp_ref[0:1, mine] * norm

    pl.semaphore_wait(barrier, 26)

    def pay_copy(k, slot):
        dy, dz = offset_of(k)
        return pltpu.make_async_remote_copy(
            src_ref=pay.at[me],
            dst_ref=pay.at[slot],
            send_sem=pay_send.at[0],
            recv_sem=pay_recv.at[slot],
            device_id=chip_at(4 - dy, 8 - dz),
            device_id_type=MESH,
        )

    for k in range(1, n_ray):
        pay_copy(k, me).start()

    loads[4].wait()
    line = lax.broadcasted_iota(jnp.int32, (rows // 2, rows // 2), 0)
    place = lax.broadcasted_iota(jnp.int32, (rows // 2, rows // 2), 1)
    flip = (line == core * place + (1 - core) * (rows // 2 - 1 - place)).astype(jnp.float32)

    def exact(left, right, dims):
        return lax.dot_general(
            left, right, dims, precision=lax.Precision.HIGHEST, preferred_element_type=jnp.float32
        )

    for wave in range(3):
        g2[core, wave] = exact(grad_ref[wave], flip, (((0,), (0,)), ((), ())))

    def g_copy(slot):
        return pltpu.make_async_remote_copy(
            src_ref=g2.at[core],
            dst_ref=g2.at[slot],
            send_sem=g_sem.at[0],
            recv_sem=g_sem.at[1],
            device_id={"pix": partner},
            device_id_type=MESH,
        )

    g_copy(core).start()

    row_start = pair * rows
    col_start = me * cols
    sub = lax.broadcasted_iota(jnp.int32, (8, half), 0)
    x_mid = (row_start + rows // 2).astype(jnp.float32) - 0.5 * NPIX
    y_mid = (col_start + cols // 2).astype(jnp.float32) - 0.5 * NPIX
    x_base = sub.astype(jnp.float32) + (0.25 * rows + 0.5)
    y_base = sub.astype(jnp.float32) + (y_mid + 0.5)
    wave_of = lax.rem(sub, 3)
    step_scale = 8.0 * jnp.where(
        wave_of == 0, wave_scales[0], jnp.where(wave_of == 1, wave_scales[1], wave_scales[2])
    )

    for wave in range(3):
        v_loc[wave][...] = jnp.zeros_like(v_loc[wave])

    def tables(block):
        rho = jnp.broadcast_to(pay[block, 0:1, :], (8, half))
        l_all = jnp.broadcast_to(pay[block, 1:2, :], (8, half))
        m_all = jnp.broadcast_to(pay[block, 2:3, :], (8, half))
        amp = jnp.broadcast_to(pay[block, 3:4, :], (8, half))
        step_c, step_s = cos_sin_turns(step_scale * jnp.where(sub < 3, l_all, m_all))
        x_turns = l_all * x_base
        y_turns = (rho + l_all * x_mid) + m_all * y_base

        def row_of(table, index):
            return jnp.broadcast_to(table[index : index + 1, :], (8, half))

        def one_wave(wave):
            scale = wave_scales[wave]

            def store_x(k, first, second):
                for part in range(2):
                    tile = jnp.concatenate([first[part], second[part]], axis=0)
                    at = part * (rows // 2) + 8 * k
                    xt[wave][block, at : at + 16, :] = tile.astype(jnp.bfloat16)

            def store_y(k, first, second):
                for part in range(2):
                    tile = jnp.concatenate([first[part], second[part]], axis=0)
                    at = part * cols + 8 * k
                    yf[wave][block, at : at + 16, :] = tile
                    yt[wave][block, at : at + 16, :] = tile.astype(jnp.bfloat16)

            ladder(
                cos_sin_turns(scale * x_turns),
                row_of(step_c, wave),
                row_of(step_s, wave),
                rows // 16,
                store_x,
            )
            bc, bs = cos_sin_turns(scale * y_turns)
            ladder(
                (amp * bc, amp * bs),
                row_of(step_c, wave + 3),
                row_of(step_s, wave + 3),
                cols // 8,
                store_y,
            )

        return one_wave

    def gather_field(block, wave):
        v_loc[wave][...] += lax.dot_general(
            yt[wave][block],
            xt[wave][block],
            (((1,), (1,)), ((), ())),
            preferred_element_type=jnp.float32,
        )

    first = tables(me)
    first(0)
    gather_field(me, 0)
    first(1)
    gather_field(me, 1)
    first(2)

    def forward_step(k, carry):
        before = block_of(k - 1)
        block = block_of(k)
        pay_copy(k, block).wait_recv()
        make = tables(block)
        gather_field(before, 2)
        make(0)
        gather_field(block, 0)
        make(1)
        gather_field(block, 1)
        make(2)
        return carry

    lax.fori_loop(1, n_ray, forward_step, 0)
    gather_field(block_of(n_ray - 1), 2)

    v_copies = [
        pltpu.make_async_remote_copy(
            src_ref=v_loc[wave],
            dst_ref=v_rem.at[wave],
            send_sem=v_sem.at[0, wave],
            recv_sem=v_sem.at[1, wave],
            device_id={"pix": partner},
            device_id_type=MESH,
        )
        for wave in range(3)
    ]
    for v_copy in v_copies:
        v_copy.start()
    g_copy(1 - core).wait_recv()

    low = lax.broadcasted_iota(jnp.int32, (cols, rows), 1) < rows // 2
    distance = (lax.broadcasted_iota(jnp.int32, (cols, rows), 1) & (rows // 2 - 1)).astype(
        jnp.float32
    ) + 0.5

    def swap(a):
        return pltpu.roll(a, rows // 2, 1)

    for wave in range(3):
        v_copies[wave].wait_recv()
        top = v_loc[wave][0:cols, :] + v_rem[wave, 0:cols, :]
        bot = v_loc[wave][cols:, :] + v_rem[wave, cols:, :]
        top_s, bot_s = swap(top), swap(bot)
        u_re = jnp.where(low, top - bot_s, top_s + bot)
        u_im = jnp.where(low, bot + top_s, bot_s - top)
        power[wave] = u_re * u_re + u_im * u_im
        weight = 2.0 * jnp.concatenate([g2[1, wave], g2[0, wave]], axis=1)
        g_re, g_im = weight * u_re, weight * u_im
        r_re, r_im = swap(g_re), swap(g_im)
        plus_re, less_re = g_re + r_re, g_re - r_re
        plus_im, less_im = g_im + r_im, g_im - r_im
        for i, table in enumerate(
            (
                jnp.where(low, plus_re, -less_im),
                jnp.where(low, plus_im, less_re),
                jnp.where(low, less_re, plus_im) * distance,
                jnp.where(low, less_im, -plus_re) * distance,
            )
        ):
            lhs[wave, i * cols : (i + 1) * cols, :] = table.astype(jnp.bfloat16)

    here = 8 * y_pos + z_pos

    def s_copy(k, far):
        dy, dz = offset_of(k)
        return pltpu.make_async_remote_copy(
            src_ref=s_snd.at[k],
            dst_ref=s_rcv.at[here],
            send_sem=s_send.at[0],
            recv_sem=s_recv.at[0],
            device_id=chip_at(dy, dz + 4 * far),
            device_id_type=MESH,
        )

    def backward(block):
        s1 = jnp.zeros((8, half), jnp.float32)
        s2 = jnp.zeros((8, half), jnp.float32)
        s3 = jnp.zeros((8, half), jnp.float32)
        s4 = jnp.zeros((8, half), jnp.float32)
        sub_f = sub.astype(jnp.float32)
        for wave in range(3):
            d_b = lax.dot_general(
                lhs[wave],
                xt[wave][block],
                (((1,), (0,)), ((), ())),
                preferred_element_type=jnp.float32,
            )
            zi = jnp.zeros((8, half), jnp.float32)
            zx = jnp.zeros((8, half), jnp.float32)
            zy = jnp.zeros((8, half), jnp.float32)
            for t in range(cols // 8):
                at = 8 * t
                br = yf[wave][block, at : at + 8, :]
                bi = yf[wave][block, cols + at : cols + at + 8, :]
                dbr = d_b[at : at + 8]
                dbi = d_b[cols + at : cols + at + 8]
                dxr = d_b[2 * cols + at : 2 * cols + at + 8]
                dxi = d_b[3 * cols + at : 3 * cols + at + 8]
                d = br * dbi - bi * dbr
                zi = zi + d
                zy = zy + d * (sub_f + (at - 0.5 * cols + 0.5))
                zx = zx + (br * dxi - bi * dxr)
                s4 = s4 + (br * dbr + bi * dbi)
            scale = wave_scales[wave]
            s1 = s1 + scale * zi
            s2 = s2 + (scale * two_pi) * (x_mid * zi + zx)
            s3 = s3 + (scale * two_pi) * (y_mid * zi + zy)
        sums = [jnp.sum(s, axis=0, keepdims=True) for s in (s1, s2, s3, s4)]
        return jnp.concatenate(
            [s[:, 128 * t : 128 * t + 128] for s in sums for t in range(half // 128)], axis=0
        )

    def backward_step(i, carry):
        k = 4 * (3 - (i & 3)) + (i >> 2)
        s_snd[k] = backward(block_of(k)).astype(jnp.bfloat16)
        s_copy(k, 1).start()

        @pl.when(k > 0)
        def _():
            s_copy(k, 0).start()

        return carry

    lax.fori_loop(0, n_ray, backward_step, 0)
    s_rcv[here] = s_snd[0]
    for wave in range(3):
        above, below = power[wave, :, : rows // 2], power[wave, :, rows // 2 :]
        psf_ref[wave] = exact(flip, jnp.where(core == 1, above, below), (((1,), (1,)), ((), ())))
    psf_store = pltpu.make_async_copy(psf_ref, psf_hbm, out_sem.at[0])
    psf_store.start()
    wait_bytes(s_rcv.at[0:31], s_recv.at[0])
    total = s_rcv[0].astype(jnp.float32)
    for b in range(1, 32):
        total = total + s_rcv[b].astype(jnp.float32)
    tot[4 * core + x_pos] = total

    for dx, other in x_others:
        pltpu.make_async_remote_copy(
            src_ref=tot.at[4 * core + x_pos],
            dst_ref=tot.at[4 * core + x_pos],
            send_sem=t_send.at[0],
            recv_sem=t_recv.at[0],
            device_id=x_peer(dx, other),
            device_id_type=MESH,
        ).start()
    wait_bytes(tot.at[0:7], t_recv.at[0])
    tiles = half // 128
    for h in range(2):
        total = tot[4 * h]
        for b in range(1, 4):
            total = total + tot[4 * h + b]
        for t in range(tiles):
            at = slice(h * half + 128 * t, h * half + 128 * t + 128)
            s1, s2, s3, s4 = (total[tiles * i + t : tiles * i + t + 1] for i in range(4))
            out_ref[0:1, at] = s1
            out_ref[1:2, at] = -two_pi * dir_ref[0:1, at] * s1
            out_ref[2:3, at] = -two_pi * dir_ref[1:2, at] * s1
            out_ref[3:4, at] = (s2 - two_pi * pos_ref[0:1, at] * s1) * (1.0 / NPIX)
            out_ref[4:5, at] = (s3 - two_pi * pos_ref[1:2, at] * s1) * (1.0 / NPIX)
            out_ref[5:6, at] = s4 / amp_ref[0:1, at]
    out_store = pltpu.make_async_copy(out_ref, out_hbm, out_sem.at[1])
    out_store.start()

    wait_bytes(pay.at[0 : n_ray - 1], pay_send.at[0])
    wait_bytes(s_rcv.at[0:31], s_send.at[0])
    wait_bytes(tot.at[0:7], t_send.at[0])
    g_copy(core).wait_send()
    for v_copy in v_copies:
        v_copy.wait_send()
    psf_store.wait()
    out_store.wait()


def on_device(n_ray, n_pix, positions, directions, path, amplitude, psf_grad):
    count = positions.shape[1]
    half = count // 2
    n_pair = n_pix // 2
    rows = NPIX // n_pair
    cols = NPIX // n_ray
    f32 = jnp.float32
    bf16 = jnp.bfloat16
    hbm_space = pl.BlockSpec(memory_space=pltpu.HBM)
    any_space = pl.BlockSpec(memory_space=pl.ANY)
    dma = pltpu.SemaphoreType.DMA
    return pl.pallas_call(
        functools.partial(kernel, n_ray, n_pix),
        out_shape=(
            jax.ShapeDtypeStruct(psf_grad.shape, f32),
            jax.ShapeDtypeStruct((6, count), f32),
        ),
        in_specs=[hbm_space] * 5,
        out_specs=(any_space, any_space),
        scratch_shapes=[
            pltpu.VMEM((2, count), f32),
            pltpu.VMEM((2, count), f32),
            pltpu.VMEM((1, count), f32),
            pltpu.VMEM((1, count), f32),
            pltpu.VMEM(psf_grad.shape, f32),
            pltpu.VMEM(psf_grad.shape, f32),
            pltpu.VMEM((6, count), f32),
            pltpu.VMEM((n_ray, 4, half), f32),
            *[pltpu.VMEM((n_ray, rows, half), bf16)] * 3,
            *[pltpu.VMEM((n_ray, 2 * cols, half), bf16)] * 3,
            *[pltpu.VMEM((n_ray, 2 * cols, half), f32)] * 3,
            *[pltpu.VMEM((2 * cols, rows), f32)] * 3,
            pltpu.VMEM((2, 3, cols, rows // 2), f32),
            pltpu.VMEM((3, 2 * cols, rows), f32),
            pltpu.VMEM((3, cols, rows), f32),
            pltpu.VMEM((3, 4 * cols, rows), bf16),
            pltpu.VMEM((n_ray, half // 32, 128), bf16),
            pltpu.VMEM((32, half // 32, 128), bf16),
            pltpu.VMEM((8, half // 32, 128), f32),
            dma((5,)),
            dma((2,)),
            dma((1,)),
            dma((n_ray,)),
            dma((2,)),
            dma((2, 3)),
            dma((1,)),
            dma((1,)),
            dma((1,)),
            dma((1,)),
        ],
        compiler_params=pltpu.CompilerParams(
            collective_id=0, has_side_effects=True, vmem_limit_bytes=48 * 1024 * 1024
        ),
        name="ray_wave",
    )(positions, directions, path.reshape(1, count), amplitude.reshape(1, count), psf_grad)


def solution(mesh):
    in_specs = (P(None, "ray"), P(None, "ray"), P("ray"), P("ray"), P(None, "pix", "ray"))
    out_specs = (P(None, "pix", "ray"), P(None, "ray"))
    body = functools.partial(on_device, mesh.shape["ray"], mesh.shape["pix"])
    return jax.shard_map(
        body, mesh=mesh, in_specs=in_specs, out_specs=out_specs, check_vma=False
    )
```

```python
import functools
import math

import jax
import jax.numpy as jnp
from jax import lax
from jax.experimental import pallas as pl
from jax.experimental.pallas import tpu as pltpu
from jax.sharding import PartitionSpec as P

NPIX = 1024

wave_scales = (1.2088, 1.0, 0.8953)
two_pi = 2.0 * math.pi
MESH = pl.DeviceIdType.MESH

COS_COEF = (
    0.9999999890590201,
    -19.739204499453688,
    64.93911745988827,
    -85.45013953077586,
    60.16763095018129,
    -25.96759924584206,
    6.528658157862129,
)
SIN_COEF = (
    6.283185302511498,
    -41.341700405316736,
    81.60513138576982,
    -76.70301535347629,
    42.02592698341473,
    -14.899846660399582,
    3.2381375010236435,
)


def horner(coef, z):
    total = coef[-1] * z + coef[-2]
    for c in coef[-3::-1]:
        total = total * z + c
    return total


def cos_sin_turns(turns):
    frac = turns - jnp.round(turns)
    z = frac * frac
    return horner(COS_COEF, z), horner(SIN_COEF, z) * frac


def ladder(base, step_c, step_s, ntiles, store):
    c0, s0 = base
    cc, ss, cs, sc = c0 * step_c, s0 * step_s, c0 * step_s, s0 * step_c
    twice = step_c + step_c
    up = (cc - ss, sc + cs)
    down = (cc + ss, sc - cs)
    mid = ntiles // 2
    store(mid, base, up)
    back, last = base, up
    for k in range(mid + 2, ntiles, 2):
        first = (twice * last[0] - back[0], twice * last[1] - back[1])
        second = (twice * first[0] - last[0], twice * first[1] - last[1])
        store(k, first, second)
        back, last = first, second
    back, last = base, down
    nxt = (twice * last[0] - back[0], twice * last[1] - back[1])
    store(mid - 2, nxt, last)
    back, last = last, nxt
    for k in range(mid - 4, -1, -2):
        second = (twice * last[0] - back[0], twice * last[1] - back[1])
        first = (twice * second[0] - last[0], twice * second[1] - last[1])
        store(k, first, second)
        back, last = second, first


def offset_of(k):
    b, a = k >> 2, k & 3
    b3, a3 = (b >> 1) * (b & 1), (a >> 1) * (a & 1)
    dy = b + (b >> 1) - 2 * b3
    dz = a + 5 * (a >> 1) - 6 * a3 + 4 * a3 * (dy & 1)
    return dy, dz


def kernel(
    n_ray,
    n_pix,
    pos_hbm,
    dir_hbm,
    path_hbm,
    amp_hbm,
    grad_hbm,
    psf_hbm,
    out_hbm,
    pos_ref,
    dir_ref,
    path_ref,
    amp_ref,
    grad_ref,
    psf_ref,
    out_ref,
    pay,
    xt0,
    xt1,
    xt2,
    yt0,
    yt1,
    yt2,
    yf0,
    yf1,
    yf2,
    v_loc0,
    v_loc1,
    v_loc2,
    g2,
    v_rem,
    power,
    lhs,
    s_snd,
    s_rcv,
    tot,
    in_sem,
    out_sem,
    pay_send,
    pay_recv,
    g_sem,
    v_sem,
    s_send,
    s_recv,
    t_send,
    t_recv,
):
    me = lax.axis_index("ray")
    pix = lax.axis_index("pix")
    xt, yt, yf, v_loc = (xt0, xt1, xt2), (yt0, yt1, yt2), (yf0, yf1, yf2), (v_loc0, v_loc1, v_loc2)
    core = pix & 1
    pair = pix >> 1
    x_pos = pair & 3
    y_pos = me >> 2
    z_pos = 4 * (pair >> 2) + (me & 3)
    n_pair = n_pix // 2
    partner = pix + 1 - 2 * core
    rows = NPIX // n_pair
    cols = NPIX // n_ray
    half = pay.shape[2]
    count = 2 * half
    norm = 1.0 / math.sqrt(count * n_ray)

    def chip_at(dy, dz):
        y = (y_pos + dy) & 3
        z = (z_pos + dz) & 7
        return {"ray": 4 * y + (z & 3), "pix": 8 * (z >> 2) + (pix & 7)}

    def block_of(k):
        dy, dz = offset_of(k)
        return 4 * ((y_pos + dy) & 3) + ((z_pos + dz) & 3)

    loads = [
        pltpu.make_async_copy(src, dst, in_sem.at[i])
        for i, (src, dst) in enumerate(
            (
                (pos_hbm, pos_ref),
                (dir_hbm, dir_ref),
                (path_hbm, path_ref),
                (amp_hbm, amp_ref),
                (grad_hbm, grad_ref),
            )
        )
    ]
    for load in loads:
        load.start()

    def wait_bytes(ref, sem):
        pltpu.make_async_copy(ref, ref, sem).wait()

    barrier = pltpu.get_barrier_semaphore()

    def x_peer(dx, other):
        return {"pix": (pix & 8) + 2 * ((x_pos + dx) & 3) + (core + other - 2 * core * other)}

    x_others = [(dx, other) for dx in range(4) for other in range(2)][1:]

    for dy, dz in [(dy, dz) for dy in range(4) for dz in (0, 1, 7, 2, 6)][1:]:
        pl.semaphore_signal(barrier, inc=1, device_id=chip_at(dy, dz), device_id_type=MESH)
    for dx, other in x_others:
        pl.semaphore_signal(barrier, inc=1, device_id=x_peer(dx, other), device_id_type=MESH)

    for load in loads[:4]:
        load.wait()
    mine = pl.ds(pl.multiple_of(core * half, 128), half)
    l_own = dir_ref[0:1, mine]
    m_own = dir_ref[1:2, mine]
    pay[me, 0:1, :] = (
        path_ref[0:1, mine] * (1.0 / two_pi) - l_own * pos_ref[0:1, mine] - m_own * pos_ref[1:2, mine]
    )
    pay[me, 1:2, :] = l_own
    pay[me, 2:3, :] = m_own
    pay[me, 3:4, :] = amp_ref[0:1, mine] * norm

    pl.semaphore_wait(barrier, 26)

    def pay_copy(k, slot):
        dy, dz = offset_of(k)
        return pltpu.make_async_remote_copy(
            src_ref=pay.at[me],
            dst_ref=pay.at[slot],
            send_sem=pay_send.at[0],
            recv_sem=pay_recv.at[slot],
            device_id=chip_at(4 - dy, 8 - dz),
            device_id_type=MESH,
        )

    for k in range(1, n_ray):
        pay_copy(k, me).start()

    loads[4].wait()
    line = lax.broadcasted_iota(jnp.int32, (rows // 2, rows // 2), 0)
    place = lax.broadcasted_iota(jnp.int32, (rows // 2, rows // 2), 1)
    flip = (line == core * place + (1 - core) * (rows // 2 - 1 - place)).astype(jnp.float32)

    def exact(left, right, dims):
        return lax.dot_general(
            left, right, dims, precision=lax.Precision.HIGHEST, preferred_element_type=jnp.float32
        )

    for wave in range(3):
        g2[core, wave] = exact(grad_ref[wave], flip, (((0,), (0,)), ((), ())))

    def g_copy(slot):
        return pltpu.make_async_remote_copy(
            src_ref=g2.at[core],
            dst_ref=g2.at[slot],
            send_sem=g_sem.at[0],
            recv_sem=g_sem.at[1],
            device_id={"pix": partner},
            device_id_type=MESH,
        )

    g_copy(core).start()

    row_start = pair * rows
    col_start = me * cols
    sub = lax.broadcasted_iota(jnp.int32, (8, half), 0)
    x_mid = (row_start + rows // 2).astype(jnp.float32) - 0.5 * NPIX
    y_mid = (col_start + cols // 2).astype(jnp.float32) - 0.5 * NPIX
    x_base = sub.astype(jnp.float32) + (0.25 * rows + 0.5)
    y_base = sub.astype(jnp.float32) + (y_mid + 0.5)
    wave_of = lax.rem(sub, 3)
    step_scale = 8.0 * jnp.where(
        wave_of == 0, wave_scales[0], jnp.where(wave_of == 1, wave_scales[1], wave_scales[2])
    )

    for wave in range(3):
        v_loc[wave][...] = jnp.zeros_like(v_loc[wave])

    def tables(block):
        rho = jnp.broadcast_to(pay[block, 0:1, :], (8, half))
        l_all = jnp.broadcast_to(pay[block, 1:2, :], (8, half))
        m_all = jnp.broadcast_to(pay[block, 2:3, :], (8, half))
        amp = jnp.broadcast_to(pay[block, 3:4, :], (8, half))
        step_c, step_s = cos_sin_turns(step_scale * jnp.where(sub < 3, l_all, m_all))
        x_turns = l_all * x_base
        y_turns = (rho + l_all * x_mid) + m_all * y_base

        def row_of(table, index):
            return jnp.broadcast_to(table[index : index + 1, :], (8, half))

        def one_wave(wave):
            scale = wave_scales[wave]

            def store_x(k, first, second):
                for part in range(2):
                    tile = jnp.concatenate([first[part], second[part]], axis=0)
                    at = part * (rows // 2) + 8 * k
                    xt[wave][block, at : at + 16, :] = tile.astype(jnp.bfloat16)

            def store_y(k, first, second):
                for part in range(2):
                    tile = jnp.concatenate([first[part], second[part]], axis=0)
                    at = part * cols + 8 * k
                    yf[wave][block, at : at + 16, :] = tile
                    yt[wave][block, at : at + 16, :] = tile.astype(jnp.bfloat16)

            ladder(
                cos_sin_turns(scale * x_turns),
                row_of(step_c, wave),
                row_of(step_s, wave),
                rows // 16,
                store_x,
            )
            bc, bs = cos_sin_turns(scale * y_turns)
            ladder(
                (amp * bc, amp * bs),
                row_of(step_c, wave + 3),
                row_of(step_s, wave + 3),
                cols // 8,
                store_y,
            )

        return one_wave

    def gather_field(block, wave):
        v_loc[wave][...] += lax.dot_general(
            yt[wave][block],
            xt[wave][block],
            (((1,), (1,)), ((), ())),
            preferred_element_type=jnp.float32,
        )

    first = tables(me)
    for wave in range(3):
        first(wave)

    def forward_step(k, carry):
        before = block_of(k - 1)
        block = block_of(k)
        pay_copy(k, block).wait_recv()
        make = tables(block)
        for wave in range(3):
            gather_field(before, wave)
        for wave in range(3):
            make(wave)
        return carry

    lax.fori_loop(1, n_ray, forward_step, 0)
    for wave in range(3):
        gather_field(block_of(n_ray - 1), wave)

    v_copies = [
        pltpu.make_async_remote_copy(
            src_ref=v_loc[wave],
            dst_ref=v_rem.at[wave],
            send_sem=v_sem.at[0, wave],
            recv_sem=v_sem.at[1, wave],
            device_id={"pix": partner},
            device_id_type=MESH,
        )
        for wave in range(3)
    ]
    for v_copy in v_copies:
        v_copy.start()
    g_copy(1 - core).wait_recv()

    low = lax.broadcasted_iota(jnp.int32, (cols, rows), 1) < rows // 2
    distance = (lax.broadcasted_iota(jnp.int32, (cols, rows), 1) & (rows // 2 - 1)).astype(
        jnp.float32
    ) + 0.5

    def swap(a):
        return pltpu.roll(a, rows // 2, 1)

    for wave in range(3):
        v_copies[wave].wait_recv()
        top = v_loc[wave][0:cols, :] + v_rem[wave, 0:cols, :]
        bot = v_loc[wave][cols:, :] + v_rem[wave, cols:, :]
        top_s, bot_s = swap(top), swap(bot)
        u_re = jnp.where(low, top - bot_s, top_s + bot)
        u_im = jnp.where(low, bot + top_s, bot_s - top)
        power[wave] = u_re * u_re + u_im * u_im
        weight = 2.0 * jnp.concatenate([g2[1, wave], g2[0, wave]], axis=1)
        g_re, g_im = weight * u_re, weight * u_im
        r_re, r_im = swap(g_re), swap(g_im)
        plus_re, less_re = g_re + r_re, g_re - r_re
        plus_im, less_im = g_im + r_im, g_im - r_im
        for i, table in enumerate(
            (
                jnp.where(low, plus_re, -less_im),
                jnp.where(low, plus_im, less_re),
                jnp.where(low, less_re, plus_im) * distance,
                jnp.where(low, less_im, -plus_re) * distance,
            )
        ):
            lhs[wave, i * cols : (i + 1) * cols, :] = table.astype(jnp.bfloat16)

    here = 8 * y_pos + z_pos

    def s_copy(k, far):
        dy, dz = offset_of(k)
        return pltpu.make_async_remote_copy(
            src_ref=s_snd.at[k],
            dst_ref=s_rcv.at[here],
            send_sem=s_send.at[0],
            recv_sem=s_recv.at[0],
            device_id=chip_at(dy, dz + 4 * far),
            device_id_type=MESH,
        )

    def backward(block):
        s1 = jnp.zeros((8, half), jnp.float32)
        s2 = jnp.zeros((8, half), jnp.float32)
        s3 = jnp.zeros((8, half), jnp.float32)
        s4 = jnp.zeros((8, half), jnp.float32)
        sub_f = sub.astype(jnp.float32)
        for wave in range(3):
            d_b = lax.dot_general(
                lhs[wave],
                xt[wave][block],
                (((1,), (0,)), ((), ())),
                preferred_element_type=jnp.float32,
            )
            zi = jnp.zeros((8, half), jnp.float32)
            zx = jnp.zeros((8, half), jnp.float32)
            zy = jnp.zeros((8, half), jnp.float32)
            for t in range(cols // 8):
                at = 8 * t
                br = yf[wave][block, at : at + 8, :]
                bi = yf[wave][block, cols + at : cols + at + 8, :]
                dbr = d_b[at : at + 8]
                dbi = d_b[cols + at : cols + at + 8]
                dxr = d_b[2 * cols + at : 2 * cols + at + 8]
                dxi = d_b[3 * cols + at : 3 * cols + at + 8]
                d = br * dbi - bi * dbr
                zi = zi + d
                zy = zy + d * (sub_f + (at - 0.5 * cols + 0.5))
                zx = zx + (br * dxi - bi * dxr)
                s4 = s4 + (br * dbr + bi * dbi)
            scale = wave_scales[wave]
            s1 = s1 + scale * zi
            s2 = s2 + (scale * two_pi) * (x_mid * zi + zx)
            s3 = s3 + (scale * two_pi) * (y_mid * zi + zy)
        sums = [jnp.sum(s, axis=0, keepdims=True) for s in (s1, s2, s3, s4)]
        return jnp.concatenate(
            [s[:, 128 * t : 128 * t + 128] for s in sums for t in range(half // 128)], axis=0
        )

    def backward_step(i, carry):
        k = 4 * (3 - (i & 3)) + (i >> 2)
        s_snd[k] = backward(block_of(k)).astype(jnp.bfloat16)
        s_copy(k, 1).start()

        @pl.when(k > 0)
        def _():
            s_copy(k, 0).start()

        return carry

    lax.fori_loop(0, n_ray, backward_step, 0)
    s_rcv[here] = s_snd[0]
    for wave in range(3):
        above, below = power[wave, :, : rows // 2], power[wave, :, rows // 2 :]
        psf_ref[wave] = exact(flip, jnp.where(core == 1, above, below), (((1,), (1,)), ((), ())))
    psf_store = pltpu.make_async_copy(psf_ref, psf_hbm, out_sem.at[0])
    psf_store.start()
    wait_bytes(s_rcv.at[0:31], s_recv.at[0])
    total = s_rcv[0].astype(jnp.float32)
    for b in range(1, 32):
        total = total + s_rcv[b].astype(jnp.float32)
    tot[4 * core + x_pos] = total

    for dx, other in x_others:
        pltpu.make_async_remote_copy(
            src_ref=tot.at[4 * core + x_pos],
            dst_ref=tot.at[4 * core + x_pos],
            send_sem=t_send.at[0],
            recv_sem=t_recv.at[0],
            device_id=x_peer(dx, other),
            device_id_type=MESH,
        ).start()
    wait_bytes(tot.at[0:7], t_recv.at[0])
    tiles = half // 128
    for h in range(2):
        total = tot[4 * h]
        for b in range(1, 4):
            total = total + tot[4 * h + b]
        for t in range(tiles):
            at = slice(h * half + 128 * t, h * half + 128 * t + 128)
            s1, s2, s3, s4 = (total[tiles * i + t : tiles * i + t + 1] for i in range(4))
            out_ref[0:1, at] = s1
            out_ref[1:2, at] = -two_pi * dir_ref[0:1, at] * s1
            out_ref[2:3, at] = -two_pi * dir_ref[1:2, at] * s1
            out_ref[3:4, at] = (s2 - two_pi * pos_ref[0:1, at] * s1) * (1.0 / NPIX)
            out_ref[4:5, at] = (s3 - two_pi * pos_ref[1:2, at] * s1) * (1.0 / NPIX)
            out_ref[5:6, at] = s4 / amp_ref[0:1, at]
    out_store = pltpu.make_async_copy(out_ref, out_hbm, out_sem.at[1])
    out_store.start()

    wait_bytes(pay.at[0 : n_ray - 1], pay_send.at[0])
    wait_bytes(s_rcv.at[0:31], s_send.at[0])
    wait_bytes(tot.at[0:7], t_send.at[0])
    g_copy(core).wait_send()
    for v_copy in v_copies:
        v_copy.wait_send()
    psf_store.wait()
    out_store.wait()


def on_device(n_ray, n_pix, positions, directions, path, amplitude, psf_grad):
    count = positions.shape[1]
    half = count // 2
    n_pair = n_pix // 2
    rows = NPIX // n_pair
    cols = NPIX // n_ray
    f32 = jnp.float32
    bf16 = jnp.bfloat16
    hbm_space = pl.BlockSpec(memory_space=pltpu.HBM)
    any_space = pl.BlockSpec(memory_space=pl.ANY)
    dma = pltpu.SemaphoreType.DMA
    return pl.pallas_call(
        functools.partial(kernel, n_ray, n_pix),
        out_shape=(
            jax.ShapeDtypeStruct(psf_grad.shape, f32),
            jax.ShapeDtypeStruct((6, count), f32),
        ),
        in_specs=[hbm_space] * 5,
        out_specs=(any_space, any_space),
        scratch_shapes=[
            pltpu.VMEM((2, count), f32),
            pltpu.VMEM((2, count), f32),
            pltpu.VMEM((1, count), f32),
            pltpu.VMEM((1, count), f32),
            pltpu.VMEM(psf_grad.shape, f32),
            pltpu.VMEM(psf_grad.shape, f32),
            pltpu.VMEM((6, count), f32),
            pltpu.VMEM((n_ray, 4, half), f32),
            *[pltpu.VMEM((n_ray, rows, half), bf16)] * 3,
            *[pltpu.VMEM((n_ray, 2 * cols, half), bf16)] * 3,
            *[pltpu.VMEM((n_ray, 2 * cols, half), f32)] * 3,
            *[pltpu.VMEM((2 * cols, rows), f32)] * 3,
            pltpu.VMEM((2, 3, cols, rows // 2), f32),
            pltpu.VMEM((3, 2 * cols, rows), f32),
            pltpu.VMEM((3, cols, rows), f32),
            pltpu.VMEM((3, 4 * cols, rows), bf16),
            pltpu.VMEM((n_ray, half // 32, 128), bf16),
            pltpu.VMEM((32, half // 32, 128), bf16),
            pltpu.VMEM((8, half // 32, 128), f32),
            dma((5,)),
            dma((2,)),
            dma((1,)),
            dma((n_ray,)),
            dma((2,)),
            dma((2, 3)),
            dma((1,)),
            dma((1,)),
            dma((1,)),
            dma((1,)),
        ],
        compiler_params=pltpu.CompilerParams(
            collective_id=0, has_side_effects=True, vmem_limit_bytes=48 * 1024 * 1024
        ),
        name="ray_wave",
    )(*[
        pltpu.with_memory_space_constraint(v, pltpu.HBM)
        for v in (positions, directions, path.reshape(1, count), amplitude.reshape(1, count), psf_grad)
    ])


def solution(mesh):
    in_specs = (P(None, "ray"), P(None, "ray"), P("ray"), P("ray"), P(None, "pix", "ray"))
    out_specs = (P(None, "pix", "ray"), P(None, "ray"))
    body = functools.partial(on_device, mesh.shape["ray"], mesh.shape["pix"])
    return jax.shard_map(
        body, mesh=mesh, in_specs=in_specs, out_specs=out_specs, check_vma=False
    )
```

```python
import functools
import math

import jax
import jax.numpy as jnp
from jax import lax
from jax.experimental import pallas as pl
from jax.experimental.pallas import tpu as pltpu
from jax.sharding import PartitionSpec as P

NPIX = 1024

wave_scales = (1.2088, 1.0, 0.8953)
two_pi = 2.0 * math.pi
MESH = pl.DeviceIdType.MESH

COS_COEF = (
    0.9999999890590201,
    -19.739204499453688,
    64.93911745988827,
    -85.45013953077586,
    60.16763095018129,
    -25.96759924584206,
    6.528658157862129,
)
SIN_COEF = (
    6.283185302511498,
    -41.341700405316736,
    81.60513138576982,
    -76.70301535347629,
    42.02592698341473,
    -14.899846660399582,
    3.2381375010236435,
)


def horner(coef, z):
    total = coef[-1] * z + coef[-2]
    for c in coef[-3::-1]:
        total = total * z + c
    return total


def cos_sin_turns(turns):
    frac = turns - jnp.round(turns)
    z = frac * frac
    return horner(COS_COEF, z), horner(SIN_COEF, z) * frac


def ladder(base, step_c, step_s, ntiles, store):
    c0, s0 = base
    cc, ss, cs, sc = c0 * step_c, s0 * step_s, c0 * step_s, s0 * step_c
    twice = step_c + step_c
    up = (cc - ss, sc + cs)
    down = (cc + ss, sc - cs)
    mid = ntiles // 2
    store(mid, base, up)
    back, last = base, up
    for k in range(mid + 2, ntiles, 2):
        first = (twice * last[0] - back[0], twice * last[1] - back[1])
        second = (twice * first[0] - last[0], twice * first[1] - last[1])
        store(k, first, second)
        back, last = first, second
    back, last = base, down
    nxt = (twice * last[0] - back[0], twice * last[1] - back[1])
    store(mid - 2, nxt, last)
    back, last = last, nxt
    for k in range(mid - 4, -1, -2):
        second = (twice * last[0] - back[0], twice * last[1] - back[1])
        first = (twice * second[0] - last[0], twice * second[1] - last[1])
        store(k, first, second)
        back, last = second, first


def offset_of(k):
    b, a = k >> 2, k & 3
    b3, a3 = (b >> 1) * (b & 1), (a >> 1) * (a & 1)
    dy = b + (b >> 1) - 2 * b3
    dz = a + 5 * (a >> 1) - 6 * a3 + 4 * a3 * (dy & 1)
    return dy, dz


def fold_row(j):
    return 8 * (j & 1) + 4 * (j >> 3 & 1) + 2 * (j >> 2 & 1) + (j >> 1 & 1)


def kernel(
    n_ray,
    n_pix,
    pos_hbm,
    dir_hbm,
    path_hbm,
    amp_hbm,
    grad_hbm,
    psf_hbm,
    out_hbm,
    pos_ref,
    dir_ref,
    path_ref,
    amp_ref,
    grad_ref,
    psf_ref,
    out_ref,
    pay,
    xt0,
    xt1,
    xt2,
    yt0,
    yt1,
    yt2,
    yf0,
    yf1,
    yf2,
    v_loc0,
    v_loc1,
    v_loc2,
    g2,
    v_rem,
    power,
    lhs,
    s_snd,
    s_rcv,
    tot,
    in_sem,
    out_sem,
    pay_send,
    pay_recv,
    g_sem,
    v_sem,
    s_send,
    s_recv,
    t_send,
    t_recv,
):
    me = lax.axis_index("ray")
    pix = lax.axis_index("pix")
    xt, yt, yf, v_loc = (xt0, xt1, xt2), (yt0, yt1, yt2), (yf0, yf1, yf2), (v_loc0, v_loc1, v_loc2)
    core = pix & 1
    pair = pix >> 1
    x_pos = pair & 3
    y_pos = me >> 2
    z_pos = 4 * (pair >> 2) + (me & 3)
    n_pair = n_pix // 2
    partner = pix + 1 - 2 * core
    rows = NPIX // n_pair
    cols = NPIX // n_ray
    half = pay.shape[2]
    count = 2 * half
    norm = 1.0 / math.sqrt(count * n_ray)

    def chip_at(dy, dz):
        y = (y_pos + dy) & 3
        z = (z_pos + dz) & 7
        return {"ray": 4 * y + (z & 3), "pix": 8 * (z >> 2) + (pix & 7)}

    def block_of(k):
        dy, dz = offset_of(k)
        return 4 * ((y_pos + dy) & 3) + ((z_pos + dz) & 3)

    loads = [
        pltpu.make_async_copy(src, dst, in_sem.at[i])
        for i, (src, dst) in enumerate(
            (
                (pos_hbm, pos_ref),
                (dir_hbm, dir_ref),
                (path_hbm, path_ref),
                (amp_hbm, amp_ref),
                (grad_hbm, grad_ref),
            )
        )
    ]
    for load in loads:
        load.start()

    def wait_bytes(ref, sem):
        pltpu.make_async_copy(ref, ref, sem).wait()

    barrier = pltpu.get_barrier_semaphore()

    def x_peer(dx, other):
        return {"pix": (pix & 8) + 2 * ((x_pos + dx) & 3) + (core + other - 2 * core * other)}

    x_others = [(dx, other) for dx in (2, 1, 3, 0) for other in range(2)][:7]
    x_others[6] = (0, 1)

    for dy, dz in [(dy, dz) for dy in range(4) for dz in (0, 1, 7, 2, 6)][1:]:
        pl.semaphore_signal(barrier, inc=1, device_id=chip_at(dy, dz), device_id_type=MESH)
    for dx, other in x_others:
        pl.semaphore_signal(barrier, inc=1, device_id=x_peer(dx, other), device_id_type=MESH)

    for load in loads[:4]:
        load.wait()
    mine = pl.ds(pl.multiple_of(core * half, 128), half)
    l_own = dir_ref[0:1, mine]
    m_own = dir_ref[1:2, mine]
    pay[me, 0:1, :] = (
        path_ref[0:1, mine] * (1.0 / two_pi) - l_own * pos_ref[0:1, mine] - m_own * pos_ref[1:2, mine]
    )
    pay[me, 1:2, :] = l_own
    pay[me, 2:3, :] = m_own
    pay[me, 3:4, :] = amp_ref[0:1, mine] * norm

    pl.semaphore_wait(barrier, 26)

    def pay_copy(k, slot):
        dy, dz = offset_of(k)
        return pltpu.make_async_remote_copy(
            src_ref=pay.at[me],
            dst_ref=pay.at[slot],
            send_sem=pay_send.at[0],
            recv_sem=pay_recv.at[slot],
            device_id=chip_at(4 - dy, 8 - dz),
            device_id_type=MESH,
        )

    for k in range(1, n_ray):
        pay_copy(k, me).start()

    loads[4].wait()
    line = lax.broadcasted_iota(jnp.int32, (rows // 2, rows // 2), 0)
    place = lax.broadcasted_iota(jnp.int32, (rows // 2, rows // 2), 1)
    flip = (line == core * place + (1 - core) * (rows // 2 - 1 - place)).astype(jnp.float32)

    def exact(left, right, dims):
        return lax.dot_general(
            left, right, dims, precision=lax.Precision.HIGHEST, preferred_element_type=jnp.float32
        )

    for wave in range(3):
        g2[core, wave] = exact(grad_ref[wave], flip, (((0,), (0,)), ((), ())))

    def g_copy(slot):
        return pltpu.make_async_remote_copy(
            src_ref=g2.at[core],
            dst_ref=g2.at[slot],
            send_sem=g_sem.at[0],
            recv_sem=g_sem.at[1],
            device_id={"pix": partner},
            device_id_type=MESH,
        )

    g_copy(core).start()

    row_start = pair * rows
    col_start = me * cols
    sub = lax.broadcasted_iota(jnp.int32, (8, half), 0)
    x_mid = (row_start + rows // 2).astype(jnp.float32) - 0.5 * NPIX
    y_mid = (col_start + cols // 2).astype(jnp.float32) - 0.5 * NPIX
    x_base = sub.astype(jnp.float32) + (0.25 * rows + 0.5)
    y_base = sub.astype(jnp.float32) + (y_mid + 0.5)
    wave_of = lax.rem(sub, 3)
    step_scale = 8.0 * jnp.where(
        wave_of == 0, wave_scales[0], jnp.where(wave_of == 1, wave_scales[1], wave_scales[2])
    )

    for wave in range(3):
        v_loc[wave][...] = jnp.zeros_like(v_loc[wave])

    def tables(block):
        rho = jnp.broadcast_to(pay[block, 0:1, :], (8, half))
        l_all = jnp.broadcast_to(pay[block, 1:2, :], (8, half))
        m_all = jnp.broadcast_to(pay[block, 2:3, :], (8, half))
        amp = jnp.broadcast_to(pay[block, 3:4, :], (8, half))
        step_c, step_s = cos_sin_turns(step_scale * jnp.where(sub < 3, l_all, m_all))
        x_turns = l_all * x_base
        y_turns = (rho + l_all * x_mid) + m_all * y_base

        def row_of(table, index):
            return jnp.broadcast_to(table[index : index + 1, :], (8, half))

        def one_wave(wave):
            scale = wave_scales[wave]

            def store_x(k, first, second):
                for part in range(2):
                    tile = jnp.concatenate([first[part], second[part]], axis=0)
                    at = part * (rows // 2) + 8 * k
                    xt[wave][block, at : at + 16, :] = tile.astype(jnp.bfloat16)

            def store_y(k, first, second):
                for part in range(2):
                    tile = jnp.concatenate([first[part], second[part]], axis=0)
                    at = part * cols + 8 * k
                    yf[wave][block, at : at + 16, :] = tile
                    yt[wave][block, at : at + 16, :] = tile.astype(jnp.bfloat16)

            ladder(
                cos_sin_turns(scale * x_turns),
                row_of(step_c, wave),
                row_of(step_s, wave),
                rows // 16,
                store_x,
            )
            bc, bs = cos_sin_turns(scale * y_turns)
            ladder(
                (amp * bc, amp * bs),
                row_of(step_c, wave + 3),
                row_of(step_s, wave + 3),
                cols // 8,
                store_y,
            )

        return one_wave

    def gather_field(block, wave, keep):
        total = v_loc[wave][...] + lax.dot_general(
            yt[wave][block],
            xt[wave][block],
            (((1,), (1,)), ((), ())),
            preferred_element_type=jnp.float32,
        )
        v_loc[wave][...] = jnp.where(keep, total, 0.0)

    def forward_step(k, carry):
        before = block_of((k - 1) & (n_ray - 1))
        block = block_of(k)

        @pl.when(k > 0)
        def _():
            pay_copy(k, block).wait_recv()

        make = tables(block)
        for wave in range(3):
            gather_field(before, wave, k > 0)
        for wave in range(3):
            make(wave)
        return carry

    lax.fori_loop(0, n_ray, forward_step, 0)
    v_copies = [
        pltpu.make_async_remote_copy(
            src_ref=v_loc[wave],
            dst_ref=v_rem.at[wave],
            send_sem=v_sem.at[0, wave],
            recv_sem=v_sem.at[1, wave],
            device_id={"pix": partner},
            device_id_type=MESH,
        )
        for wave in range(3)
    ]
    for wave in range(3):
        gather_field(block_of(n_ray - 1), wave, True)
        v_copies[wave].start()
    g_copy(1 - core).wait_recv()

    low = lax.broadcasted_iota(jnp.int32, (cols, rows), 1) < rows // 2
    distance = (lax.broadcasted_iota(jnp.int32, (cols, rows), 1) & (rows // 2 - 1)).astype(
        jnp.float32
    ) + 0.5

    def swap(a):
        return pltpu.roll(a, rows // 2, 1)

    for wave in range(3):
        v_copies[wave].wait_recv()
        top = v_loc[wave][0:cols, :] + v_rem[wave, 0:cols, :]
        bot = v_loc[wave][cols:, :] + v_rem[wave, cols:, :]
        top_s, bot_s = swap(top), swap(bot)
        u_re = jnp.where(low, top - bot_s, top_s + bot)
        u_im = jnp.where(low, bot + top_s, bot_s - top)
        power[wave] = u_re * u_re + u_im * u_im
        weight = 2.0 * jnp.concatenate([g2[1, wave], g2[0, wave]], axis=1)
        g_re, g_im = weight * u_re, weight * u_im
        r_re, r_im = swap(g_re), swap(g_im)
        plus_re, less_re = g_re + r_re, g_re - r_re
        plus_im, less_im = g_im + r_im, g_im - r_im
        for i, table in enumerate(
            (
                jnp.where(low, plus_re, -less_im),
                jnp.where(low, plus_im, less_re),
                jnp.where(low, less_re, plus_im) * distance,
                jnp.where(low, less_im, -plus_re) * distance,
            )
        ):
            lhs[wave, i * cols : (i + 1) * cols, :] = table.astype(jnp.bfloat16)

    here = 8 * y_pos + z_pos

    def s_copy(k, far):
        dy, dz = offset_of(k)
        return pltpu.make_async_remote_copy(
            src_ref=s_snd.at[k],
            dst_ref=s_rcv.at[here],
            send_sem=s_send.at[0],
            recv_sem=s_recv.at[0],
            device_id=chip_at(dy, dz + 4 * far),
            device_id_type=MESH,
        )

    def project(block, wave):
        return lax.dot_general(
            lhs[wave],
            xt[wave][block],
            (((1,), (0,)), ((), ())),
            preferred_element_type=jnp.float32,
        )

    sub_f = sub.astype(jnp.float32)

    def contract(block, wave, sums):
        d_wave = project(block, wave)
        s1, s2, s3, s4 = sums
        zi = zx = zy = None
        for t in range(cols // 8):
            at = 8 * t
            br = yf[wave][block, at : at + 8, :]
            bi = yf[wave][block, cols + at : cols + at + 8, :]
            dbr = d_wave[at : at + 8, :]
            dbi = d_wave[cols + at : cols + at + 8, :]
            dxr = d_wave[2 * cols + at : 2 * cols + at + 8, :]
            dxi = d_wave[3 * cols + at : 3 * cols + at + 8, :]
            d = br * dbi - bi * dbr
            dx = br * dxi - bi * dxr
            dy = d * (sub_f + (at - 0.5 * cols + 0.5))
            s4 = s4 + (br * dbr + bi * dbi)
            zi, zx, zy = (d, dx, dy) if t == 0 else (zi + d, zx + dx, zy + dy)
        scale = wave_scales[wave]
        s1 = s1 + scale * zi
        s2 = s2 + (scale * two_pi) * (x_mid * zi + zx)
        s3 = s3 + (scale * two_pi) * (y_mid * zi + zy)
        return s1, s2, s3, s4

    def order(i):
        a = (i >> 2) & 3
        return 4 * ((3 + ((4 - a) >> 2) - (i & 3)) & 3) + a

    def fold(tiles):
        lane_row = lax.broadcasted_iota(jnp.int32, (8, 128), 0)
        for shift in (4, 2, 1):
            keep = (lane_row & shift) == 0
            n = len(tiles) // 2
            tiles = [
                jnp.where(keep, a + pltpu.roll(a, 8 - shift, 0), b + pltpu.roll(b, shift, 0))
                for a, b in zip(tiles[:n], tiles[n:])
            ]
        return jnp.concatenate(tiles, axis=0)

    def one_block(k, block):
        sums = (jnp.zeros((8, half), jnp.float32),) * 4
        for wave in range(3):
            sums = contract(block, wave, sums)
        tiles = [s[:, 128 * t : 128 * t + 128] for s in sums for t in range(half // 128)]
        s_snd[k] = fold(tiles).astype(jnp.bfloat16)

    def backward_step(i, carry):
        ks = [order(2 * i + n) for n in range(2)]
        for k in ks:
            one_block(k, block_of(k))
        for k in ks:
            s_copy(k, 1).start()

        @pl.when(i > 0)
        def _():
            s_copy(ks[0], 0).start()

        s_copy(ks[1], 0).start()
        return carry

    lax.fori_loop(0, n_ray // 2, backward_step, 0)
    s_rcv[here] = s_snd[0]
    for wave in range(3):
        above, below = power[wave, :, : rows // 2], power[wave, :, rows // 2 :]
        psf_ref[wave] = exact(flip, jnp.where(core == 1, above, below), (((1,), (1,)), ((), ())))
    psf_store = pltpu.make_async_copy(psf_ref, psf_hbm, out_sem.at[0])
    psf_store.start()
    wait_bytes(s_rcv.at[0:31], s_recv.at[0])
    total = s_rcv[0].astype(jnp.float32)
    for b in range(1, 32):
        total = total + s_rcv[b].astype(jnp.float32)
    tot[4 * core + x_pos] = total

    for dx, other in x_others:
        pltpu.make_async_remote_copy(
            src_ref=tot.at[4 * core + x_pos],
            dst_ref=tot.at[4 * core + x_pos],
            send_sem=t_send.at[0],
            recv_sem=t_recv.at[0],
            device_id=x_peer(dx, other),
            device_id_type=MESH,
        ).start()
    wait_bytes(tot.at[0:7], t_recv.at[0])
    tiles = half // 128
    for h in range(2):
        total = tot[4 * h]
        for b in range(1, 4):
            total = total + tot[4 * h + b]
        for t in range(tiles):
            at = slice(h * half + 128 * t, h * half + 128 * t + 128)
            s1, s2, s3, s4 = (total[r : r + 1] for r in (fold_row(tiles * i + t) for i in range(4)))
            out_ref[0:1, at] = s1
            out_ref[1:2, at] = -two_pi * dir_ref[0:1, at] * s1
            out_ref[2:3, at] = -two_pi * dir_ref[1:2, at] * s1
            out_ref[3:4, at] = (s2 - two_pi * pos_ref[0:1, at] * s1) * (1.0 / NPIX)
            out_ref[4:5, at] = (s3 - two_pi * pos_ref[1:2, at] * s1) * (1.0 / NPIX)
            out_ref[5:6, at] = s4 / amp_ref[0:1, at]
    out_store = pltpu.make_async_copy(out_ref, out_hbm, out_sem.at[1])
    out_store.start()

    wait_bytes(pay.at[0 : n_ray - 1], pay_send.at[0])
    wait_bytes(s_rcv.at[0:31], s_send.at[0])
    wait_bytes(tot.at[0:7], t_send.at[0])
    g_copy(core).wait_send()
    for v_copy in v_copies:
        v_copy.wait_send()
    psf_store.wait()
    out_store.wait()


def on_device(n_ray, n_pix, positions, directions, path, amplitude, psf_grad):
    count = positions.shape[1]
    half = count // 2
    n_pair = n_pix // 2
    rows = NPIX // n_pair
    cols = NPIX // n_ray
    f32 = jnp.float32
    bf16 = jnp.bfloat16
    hbm_space = pl.BlockSpec(memory_space=pltpu.HBM)
    any_space = pl.BlockSpec(memory_space=pl.ANY)
    dma = pltpu.SemaphoreType.DMA
    return pl.pallas_call(
        functools.partial(kernel, n_ray, n_pix),
        out_shape=(
            jax.ShapeDtypeStruct(psf_grad.shape, f32),
            jax.ShapeDtypeStruct((6, count), f32),
        ),
        in_specs=[hbm_space] * 5,
        out_specs=(any_space, any_space),
        scratch_shapes=[
            pltpu.VMEM((2, count), f32),
            pltpu.VMEM((2, count), f32),
            pltpu.VMEM((1, count), f32),
            pltpu.VMEM((1, count), f32),
            pltpu.VMEM(psf_grad.shape, f32),
            pltpu.VMEM(psf_grad.shape, f32),
            pltpu.VMEM((6, count), f32),
            pltpu.VMEM((n_ray, 4, half), f32),
            *[pltpu.VMEM((n_ray, rows, half), bf16)] * 3,
            *[pltpu.VMEM((n_ray, 2 * cols, half), bf16)] * 3,
            *[pltpu.VMEM((n_ray, 2 * cols, half), f32)] * 3,
            *[pltpu.VMEM((2 * cols, rows), f32)] * 3,
            pltpu.VMEM((2, 3, cols, rows // 2), f32),
            pltpu.VMEM((3, 2 * cols, rows), f32),
            pltpu.VMEM((3, cols, rows), f32),
            pltpu.VMEM((3, 4 * cols, rows), bf16),
            pltpu.VMEM((n_ray, half // 32, 128), bf16),
            pltpu.VMEM((32, half // 32, 128), bf16),
            pltpu.VMEM((8, half // 32, 128), f32),
            dma((5,)),
            dma((2,)),
            dma((1,)),
            dma((n_ray,)),
            dma((2,)),
            dma((2, 3)),
            dma((1,)),
            dma((1,)),
            dma((1,)),
            dma((1,)),
        ],
        compiler_params=pltpu.CompilerParams(
            collective_id=0, has_side_effects=True, vmem_limit_bytes=48 * 1024 * 1024
        ),
        name="ray_wave",
    )(*[
        pltpu.with_memory_space_constraint(v, pltpu.HBM)
        for v in (positions, directions, path.reshape(1, count), amplitude.reshape(1, count), psf_grad)
    ])


def solution(mesh):
    in_specs = (P(None, "ray"), P(None, "ray"), P("ray"), P("ray"), P(None, "pix", "ray"))
    out_specs = (P(None, "pix", "ray"), P(None, "ray"))
    body = functools.partial(on_device, mesh.shape["ray"], mesh.shape["pix"])
    return jax.shard_map(
        body, mesh=mesh, in_specs=in_specs, out_specs=out_specs, check_vma=False
    )
```

```python
import functools
import math

import jax
import jax.numpy as jnp
from jax import lax
from jax.experimental import pallas as pl
from jax.experimental.pallas import tpu as pltpu
from jax.sharding import PartitionSpec as P

NPIX = 1024

wave_scales = (1.2088, 1.0, 0.8953)
two_pi = 2.0 * math.pi
MESH = pl.DeviceIdType.MESH

COS_COEF = (
    0.9999999890590201,
    -19.739204499453688,
    64.93911745988827,
    -85.45013953077586,
    60.16763095018129,
    -25.96759924584206,
    6.528658157862129,
)
SIN_COEF = (
    6.283185302511498,
    -41.341700405316736,
    81.60513138576982,
    -76.70301535347629,
    42.02592698341473,
    -14.899846660399582,
    3.2381375010236435,
)


def horner(coef, z):
    total = coef[-1] * z + coef[-2]
    for c in coef[-3::-1]:
        total = total * z + c
    return total


def cos_sin_turns(turns):
    frac = turns - jnp.round(turns)
    z = frac * frac
    return horner(COS_COEF, z), horner(SIN_COEF, z) * frac


def ladder(base, step_c, step_s, ntiles, store):
    c0, s0 = base
    cc, ss, cs, sc = c0 * step_c, s0 * step_s, c0 * step_s, s0 * step_c
    twice = step_c + step_c
    up = (cc - ss, sc + cs)
    down = (cc + ss, sc - cs)
    mid = ntiles // 2
    store(mid, base, up)
    back, last = base, up
    for k in range(mid + 2, ntiles, 2):
        first = (twice * last[0] - back[0], twice * last[1] - back[1])
        second = (twice * first[0] - last[0], twice * first[1] - last[1])
        store(k, first, second)
        back, last = first, second
    back, last = base, down
    nxt = (twice * last[0] - back[0], twice * last[1] - back[1])
    store(mid - 2, nxt, last)
    back, last = last, nxt
    for k in range(mid - 4, -1, -2):
        second = (twice * last[0] - back[0], twice * last[1] - back[1])
        first = (twice * second[0] - last[0], twice * second[1] - last[1])
        store(k, first, second)
        back, last = second, first


def offset_of(k):
    b, a = k >> 2, k & 3
    b3, a3 = (b >> 1) * (b & 1), (a >> 1) * (a & 1)
    dy = b + (b >> 1) - 2 * b3
    dz = a + 5 * (a >> 1) - 6 * a3 + 4 * a3 * (dy & 1)
    return dy, dz


def fold_row(j):
    return 8 * (j & 1) + 4 * (j >> 3 & 1) + 2 * (j >> 2 & 1) + (j >> 1 & 1)


def kernel(
    n_ray,
    n_pix,
    pos_hbm,
    dir_hbm,
    path_hbm,
    amp_hbm,
    grad_hbm,
    psf_hbm,
    out_hbm,
    pos_ref,
    dir_ref,
    path_ref,
    amp_ref,
    grad_ref,
    psf_ref,
    out_ref,
    pay,
    xt0,
    xt1,
    xt2,
    yt0,
    yt1,
    yt2,
    yf0,
    yf1,
    yf2,
    v_loc0,
    v_loc1,
    v_loc2,
    g2,
    v_rem,
    power,
    lhs,
    s_snd,
    s_rcv,
    tot,
    in_sem,
    out_sem,
    pay_send,
    pay_recv,
    g_sem,
    v_sem,
    s_send,
    s_recv,
    t_send,
    t_recv,
):
    me = lax.axis_index("ray")
    pix = lax.axis_index("pix")
    xt, yt, yf, v_loc = (xt0, xt1, xt2), (yt0, yt1, yt2), (yf0, yf1, yf2), (v_loc0, v_loc1, v_loc2)
    core = pix & 1
    pair = pix >> 1
    x_pos = pair & 3
    y_pos = me >> 2
    z_pos = 4 * (pair >> 2) + (me & 3)
    n_pair = n_pix // 2
    partner = pix + 1 - 2 * core
    rows = NPIX // n_pair
    cols = NPIX // n_ray
    half = pay.shape[2]
    count = 2 * half
    norm = 1.0 / math.sqrt(count * n_ray)

    def chip_at(dy, dz):
        y = (y_pos + dy) & 3
        z = (z_pos + dz) & 7
        return {"ray": 4 * y + (z & 3), "pix": 8 * (z >> 2) + (pix & 7)}

    def block_of(k):
        dy, dz = offset_of(k)
        return 4 * ((y_pos + dy) & 3) + ((z_pos + dz) & 3)

    loads = [
        pltpu.make_async_copy(src, dst, in_sem.at[i])
        for i, (src, dst) in enumerate(
            (
                (pos_hbm, pos_ref),
                (dir_hbm, dir_ref),
                (path_hbm, path_ref),
                (amp_hbm, amp_ref),
                (grad_hbm, grad_ref),
            )
        )
    ]
    for load in loads:
        load.start()

    def wait_bytes(ref, sem):
        pltpu.make_async_copy(ref, ref, sem).wait()

    barrier = pltpu.get_barrier_semaphore()

    def x_peer(dx, other):
        return {"pix": (pix & 8) + 2 * ((x_pos + dx) & 3) + (core + other - 2 * core * other)}

    x_others = [(dx, other) for dx in (2, 1, 3, 0) for other in range(2)][:7]
    x_others[6] = (0, 1)

    for dy, dz in ((2, 2), (2, 6), (1, 2), (1, 6), (2, 1), (2, 7), (3, 2), (3, 6), (0, 2), (0, 6), (1, 1), (1, 7), (2, 0), (3, 1), (3, 7), (0, 1), (0, 7), (1, 0), (3, 0)):
        pl.semaphore_signal(barrier, inc=1, device_id=chip_at(dy, dz), device_id_type=MESH)
    for dx, other in x_others:
        pl.semaphore_signal(barrier, inc=1, device_id=x_peer(dx, other), device_id_type=MESH)

    for load in loads[:4]:
        load.wait()
    mine = pl.ds(pl.multiple_of(core * half, 128), half)
    l_own = dir_ref[0:1, mine]
    m_own = dir_ref[1:2, mine]
    pay[me, 0:1, :] = (
        path_ref[0:1, mine] * (1.0 / two_pi) - l_own * pos_ref[0:1, mine] - m_own * pos_ref[1:2, mine]
    )
    pay[me, 1:2, :] = l_own
    pay[me, 2:3, :] = m_own
    pay[me, 3:4, :] = amp_ref[0:1, mine] * norm

    pl.semaphore_wait(barrier, 26)

    def pay_copy(k, slot):
        dy, dz = offset_of(k)
        return pltpu.make_async_remote_copy(
            src_ref=pay.at[me],
            dst_ref=pay.at[slot],
            send_sem=pay_send.at[0],
            recv_sem=pay_recv.at[slot],
            device_id=chip_at(4 - dy, 8 - dz),
            device_id_type=MESH,
        )

    for k in range(1, n_ray):
        pay_copy(k, me).start()

    loads[4].wait()
    line = lax.broadcasted_iota(jnp.int32, (rows // 2, rows // 2), 0)
    place = lax.broadcasted_iota(jnp.int32, (rows // 2, rows // 2), 1)
    flip = (line == core * place + (1 - core) * (rows // 2 - 1 - place)).astype(jnp.float32)

    def exact(left, right, dims):
        return lax.dot_general(
            left, right, dims, precision=lax.Precision.HIGHEST, preferred_element_type=jnp.float32
        )

    for wave in range(3):
        g2[core, wave] = exact(grad_ref[wave], flip, (((0,), (0,)), ((), ())))

    def g_copy(slot):
        return pltpu.make_async_remote_copy(
            src_ref=g2.at[core],
            dst_ref=g2.at[slot],
            send_sem=g_sem.at[0],
            recv_sem=g_sem.at[1],
            device_id={"pix": partner},
            device_id_type=MESH,
        )

    g_copy(core).start()

    row_start = pair * rows
    col_start = me * cols
    sub = lax.broadcasted_iota(jnp.int32, (8, half), 0)
    x_mid = (row_start + rows // 2).astype(jnp.float32) - 0.5 * NPIX
    y_mid = (col_start + cols // 2).astype(jnp.float32) - 0.5 * NPIX
    x_base = sub.astype(jnp.float32) + (0.25 * rows + 0.5)
    y_base = sub.astype(jnp.float32) + (y_mid + 0.5)
    wave_of = lax.rem(sub, 3)
    step_scale = 8.0 * jnp.where(
        wave_of == 0, wave_scales[0], jnp.where(wave_of == 1, wave_scales[1], wave_scales[2])
    )

    for wave in range(3):
        v_loc[wave][...] = jnp.zeros_like(v_loc[wave])

    def tables(block):
        rho = jnp.broadcast_to(pay[block, 0:1, :], (8, half))
        l_all = jnp.broadcast_to(pay[block, 1:2, :], (8, half))
        m_all = jnp.broadcast_to(pay[block, 2:3, :], (8, half))
        amp = jnp.broadcast_to(pay[block, 3:4, :], (8, half))
        step_c, step_s = cos_sin_turns(step_scale * jnp.where(sub < 3, l_all, m_all))
        x_turns = l_all * x_base
        y_turns = (rho + l_all * x_mid) + m_all * y_base

        def row_of(table, index):
            return jnp.broadcast_to(table[index : index + 1, :], (8, half))

        def one_wave(wave):
            scale = wave_scales[wave]

            def store_x(k, first, second):
                for part in range(2):
                    tile = jnp.concatenate([first[part], second[part]], axis=0)
                    at = part * (rows // 2) + 8 * k
                    xt[wave][block, at : at + 16, :] = tile.astype(jnp.bfloat16)

            def store_y(k, first, second):
                for part in range(2):
                    tile = jnp.concatenate([first[part], second[part]], axis=0)
                    at = part * cols + 8 * k
                    yf[wave][block, at : at + 16, :] = tile
                    yt[wave][block, at : at + 16, :] = tile.astype(jnp.bfloat16)

            ladder(
                cos_sin_turns(scale * x_turns),
                row_of(step_c, wave),
                row_of(step_s, wave),
                rows // 16,
                store_x,
            )
            bc, bs = cos_sin_turns(scale * y_turns)
            ladder(
                (amp * bc, amp * bs),
                row_of(step_c, wave + 3),
                row_of(step_s, wave + 3),
                cols // 8,
                store_y,
            )

        return one_wave

    def gather_field(block, wave, keep):
        total = v_loc[wave][...] + lax.dot_general(
            yt[wave][block],
            xt[wave][block],
            (((1,), (1,)), ((), ())),
            preferred_element_type=jnp.float32,
        )
        v_loc[wave][...] = jnp.where(keep, total, 0.0)

    def forward_step(k, carry):
        before = block_of((k - 1) & (n_ray - 1))
        block = block_of(k)

        @pl.when(k > 0)
        def _():
            pay_copy(k, block).wait_recv()

        make = tables(block)
        for wave in range(3):
            gather_field(before, wave, k > 0)
        for wave in range(3):
            make(wave)
        return carry

    lax.fori_loop(0, n_ray, forward_step, 0)
    v_copies = [
        pltpu.make_async_remote_copy(
            src_ref=v_loc[wave],
            dst_ref=v_rem.at[wave],
            send_sem=v_sem.at[0, wave],
            recv_sem=v_sem.at[1, wave],
            device_id={"pix": partner},
            device_id_type=MESH,
        )
        for wave in range(3)
    ]
    for wave in range(3):
        gather_field(block_of(n_ray - 1), wave, True)
        v_copies[wave].start()
    g_copy(1 - core).wait_recv()

    low = lax.broadcasted_iota(jnp.int32, (cols, rows), 1) < rows // 2
    distance = (lax.broadcasted_iota(jnp.int32, (cols, rows), 1) & (rows // 2 - 1)).astype(
        jnp.float32
    ) + 0.5

    def swap(a):
        return pltpu.roll(a, rows // 2, 1)

    for wave in range(3):
        v_copies[wave].wait_recv()
        top = v_loc[wave][0:cols, :] + v_rem[wave, 0:cols, :]
        bot = v_loc[wave][cols:, :] + v_rem[wave, cols:, :]
        top_s, bot_s = swap(top), swap(bot)
        u_re = jnp.where(low, top - bot_s, top_s + bot)
        u_im = jnp.where(low, bot + top_s, bot_s - top)
        power[wave] = u_re * u_re + u_im * u_im
        weight = 2.0 * jnp.concatenate([g2[1, wave], g2[0, wave]], axis=1)
        g_re, g_im = weight * u_re, weight * u_im
        r_re, r_im = swap(g_re), swap(g_im)
        plus_re, less_re = g_re + r_re, g_re - r_re
        plus_im, less_im = g_im + r_im, g_im - r_im
        for i, table in enumerate(
            (
                jnp.where(low, plus_re, -less_im),
                jnp.where(low, plus_im, less_re),
                jnp.where(low, less_re, plus_im) * distance,
                jnp.where(low, less_im, -plus_re) * distance,
            )
        ):
            lhs[wave, i * cols : (i + 1) * cols, :] = table.astype(jnp.bfloat16)

    here = 8 * y_pos + z_pos

    def s_copy(k, far):
        dy, dz = offset_of(k)
        return pltpu.make_async_remote_copy(
            src_ref=s_snd.at[k],
            dst_ref=s_rcv.at[here],
            send_sem=s_send.at[0],
            recv_sem=s_recv.at[0],
            device_id=chip_at(dy, dz + 4 * far),
            device_id_type=MESH,
        )

    def project(block, wave):
        return lax.dot_general(
            lhs[wave],
            xt[wave][block],
            (((1,), (0,)), ((), ())),
            preferred_element_type=jnp.float32,
        )

    sub_f = sub.astype(jnp.float32)

    def contract(block, wave, sums):
        d_wave = project(block, wave)
        s1, s2, s3, s4 = sums
        zi = zx = zy = None
        for t in range(cols // 8):
            at = 8 * t
            br = yf[wave][block, at : at + 8, :]
            bi = yf[wave][block, cols + at : cols + at + 8, :]
            dbr = d_wave[at : at + 8, :]
            dbi = d_wave[cols + at : cols + at + 8, :]
            dxr = d_wave[2 * cols + at : 2 * cols + at + 8, :]
            dxi = d_wave[3 * cols + at : 3 * cols + at + 8, :]
            d = br * dbi - bi * dbr
            dx = br * dxi - bi * dxr
            dy = d * (sub_f + (at - 0.5 * cols + 0.5))
            s4 = s4 + (br * dbr + bi * dbi)
            zi, zx, zy = (d, dx, dy) if t == 0 else (zi + d, zx + dx, zy + dy)
        scale = wave_scales[wave]
        s1 = s1 + scale * zi
        s2 = s2 + (scale * two_pi) * (x_mid * zi + zx)
        s3 = s3 + (scale * two_pi) * (y_mid * zi + zy)
        return s1, s2, s3, s4

    def order(i):
        a = (i >> 2) & 3
        return 4 * ((3 + ((4 - a) >> 2) - (i & 3)) & 3) + a

    def fold(tiles):
        lane_row = lax.broadcasted_iota(jnp.int32, (8, 128), 0)
        for shift in (4, 2, 1):
            keep = (lane_row & shift) == 0
            n = len(tiles) // 2
            tiles = [
                jnp.where(keep, a + pltpu.roll(a, 8 - shift, 0), b + pltpu.roll(b, shift, 0))
                for a, b in zip(tiles[:n], tiles[n:])
            ]
        return jnp.concatenate(tiles, axis=0)

    def one_block(k, block):
        sums = (jnp.zeros((8, half), jnp.float32),) * 4
        for wave in range(3):
            sums = contract(block, wave, sums)
        tiles = [s[:, 128 * t : 128 * t + 128] for s in sums for t in range(half // 128)]
        s_snd[k] = fold(tiles).astype(jnp.bfloat16)

    def backward_step(i, carry):
        ks = [order(2 * i + n) for n in range(2)]
        for k in ks:
            one_block(k, block_of(k))
        for k in ks:
            s_copy(k, 1).start()

        @pl.when(i > 0)
        def _():
            s_copy(ks[0], 0).start()

        s_copy(ks[1], 0).start()
        return carry

    lax.fori_loop(0, n_ray // 2, backward_step, 0)
    s_rcv[here] = s_snd[0]
    for wave in range(3):
        above, below = power[wave, :, : rows // 2], power[wave, :, rows // 2 :]
        psf_ref[wave] = exact(flip, jnp.where(core == 1, above, below), (((1,), (1,)), ((), ())))
    psf_store = pltpu.make_async_copy(psf_ref, psf_hbm, out_sem.at[0])
    psf_store.start()
    wait_bytes(s_rcv.at[0:31], s_recv.at[0])
    total = s_rcv[0].astype(jnp.float32)
    for b in range(1, 32):
        total = total + s_rcv[b].astype(jnp.float32)
    tot[4 * core + x_pos] = total

    for dx, other in x_others:
        pltpu.make_async_remote_copy(
            src_ref=tot.at[4 * core + x_pos],
            dst_ref=tot.at[4 * core + x_pos],
            send_sem=t_send.at[0],
            recv_sem=t_recv.at[0],
            device_id=x_peer(dx, other),
            device_id_type=MESH,
        ).start()
    wait_bytes(tot.at[0:7], t_recv.at[0])
    tiles = half // 128
    for h in range(2):
        total = tot[4 * h]
        for b in range(1, 4):
            total = total + tot[4 * h + b]
        for t in range(tiles):
            at = slice(h * half + 128 * t, h * half + 128 * t + 128)
            s1, s2, s3, s4 = (total[r : r + 1] for r in (fold_row(tiles * i + t) for i in range(4)))
            out_ref[0:1, at] = s1
            out_ref[1:2, at] = -two_pi * dir_ref[0:1, at] * s1
            out_ref[2:3, at] = -two_pi * dir_ref[1:2, at] * s1
            out_ref[3:4, at] = (s2 - two_pi * pos_ref[0:1, at] * s1) * (1.0 / NPIX)
            out_ref[4:5, at] = (s3 - two_pi * pos_ref[1:2, at] * s1) * (1.0 / NPIX)
            out_ref[5:6, at] = s4 / amp_ref[0:1, at]
    out_store = pltpu.make_async_copy(out_ref, out_hbm, out_sem.at[1])
    out_store.start()

    wait_bytes(pay.at[0 : n_ray - 1], pay_send.at[0])
    wait_bytes(s_rcv.at[0:31], s_send.at[0])
    wait_bytes(tot.at[0:7], t_send.at[0])
    g_copy(core).wait_send()
    for v_copy in v_copies:
        v_copy.wait_send()
    psf_store.wait()
    out_store.wait()


def on_device(n_ray, n_pix, positions, directions, path, amplitude, psf_grad):
    count = positions.shape[1]
    half = count // 2
    n_pair = n_pix // 2
    rows = NPIX // n_pair
    cols = NPIX // n_ray
    f32 = jnp.float32
    bf16 = jnp.bfloat16
    hbm_space = pl.BlockSpec(memory_space=pltpu.HBM)
    any_space = pl.BlockSpec(memory_space=pl.ANY)
    dma = pltpu.SemaphoreType.DMA
    return pl.pallas_call(
        functools.partial(kernel, n_ray, n_pix),
        out_shape=(
            jax.ShapeDtypeStruct(psf_grad.shape, f32),
            jax.ShapeDtypeStruct((6, count), f32),
        ),
        in_specs=[hbm_space] * 5,
        out_specs=(any_space, any_space),
        scratch_shapes=[
            pltpu.VMEM((2, count), f32),
            pltpu.VMEM((2, count), f32),
            pltpu.VMEM((1, count), f32),
            pltpu.VMEM((1, count), f32),
            pltpu.VMEM(psf_grad.shape, f32),
            pltpu.VMEM(psf_grad.shape, f32),
            pltpu.VMEM((6, count), f32),
            pltpu.VMEM((n_ray, 4, half), f32),
            *[pltpu.VMEM((n_ray, rows, half), bf16)] * 3,
            *[pltpu.VMEM((n_ray, 2 * cols, half), bf16)] * 3,
            *[pltpu.VMEM((n_ray, 2 * cols, half), f32)] * 3,
            *[pltpu.VMEM((2 * cols, rows), f32)] * 3,
            pltpu.VMEM((2, 3, cols, rows // 2), f32),
            pltpu.VMEM((3, 2 * cols, rows), f32),
            pltpu.VMEM((3, cols, rows), f32),
            pltpu.VMEM((3, 4 * cols, rows), bf16),
            pltpu.VMEM((n_ray, half // 32, 128), bf16),
            pltpu.VMEM((32, half // 32, 128), bf16),
            pltpu.VMEM((8, half // 32, 128), f32),
            dma((5,)),
            dma((2,)),
            dma((1,)),
            dma((n_ray,)),
            dma((2,)),
            dma((2, 3)),
            dma((1,)),
            dma((1,)),
            dma((1,)),
            dma((1,)),
        ],
        compiler_params=pltpu.CompilerParams(
            collective_id=0, has_side_effects=True, vmem_limit_bytes=48 * 1024 * 1024
        ),
        name="ray_wave",
    )(*[
        pltpu.with_memory_space_constraint(v, pltpu.HBM)
        for v in (positions, directions, path.reshape(1, count), amplitude.reshape(1, count), psf_grad)
    ])


def solution(mesh):
    in_specs = (P(None, "ray"), P(None, "ray"), P("ray"), P("ray"), P(None, "pix", "ray"))
    out_specs = (P(None, "pix", "ray"), P(None, "ray"))
    body = functools.partial(on_device, mesh.shape["ray"], mesh.shape["pix"])
    return jax.shard_map(
        body, mesh=mesh, in_specs=in_specs, out_specs=out_specs, check_vma=False
    )
```

```python
import functools
import math

import jax
import jax.numpy as jnp
from jax import lax
from jax.experimental import pallas as pl
from jax.experimental.pallas import tpu as pltpu
from jax.sharding import PartitionSpec as P

NPIX = 1024

wave_scales = (1.2088, 1.0, 0.8953)
two_pi = 2.0 * math.pi
MESH = pl.DeviceIdType.MESH

COS_COEF = (
    0.9999999890590201,
    -19.739204499453688,
    64.93911745988827,
    -85.45013953077586,
    60.16763095018129,
    -25.96759924584206,
    6.528658157862129,
)
SIN_COEF = (
    6.283185302511498,
    -41.341700405316736,
    81.60513138576982,
    -76.70301535347629,
    42.02592698341473,
    -14.899846660399582,
    3.2381375010236435,
)


def horner(coef, z):
    total = coef[-1] * z + coef[-2]
    for c in coef[-3::-1]:
        total = total * z + c
    return total


def cos_sin_turns(turns):
    frac = turns - jnp.round(turns)
    z = frac * frac
    return horner(COS_COEF, z), horner(SIN_COEF, z) * frac


def ladder(base, step_c, step_s, ntiles, store):
    c0, s0 = base
    cc, ss, cs, sc = c0 * step_c, s0 * step_s, c0 * step_s, s0 * step_c
    twice = step_c + step_c
    up = (cc - ss, sc + cs)
    down = (cc + ss, sc - cs)
    mid = ntiles // 2
    store(mid, base, up)
    back, last = base, up
    for k in range(mid + 2, ntiles, 2):
        first = (twice * last[0] - back[0], twice * last[1] - back[1])
        second = (twice * first[0] - last[0], twice * first[1] - last[1])
        store(k, first, second)
        back, last = first, second
    back, last = base, down
    nxt = (twice * last[0] - back[0], twice * last[1] - back[1])
    store(mid - 2, nxt, last)
    back, last = last, nxt
    for k in range(mid - 4, -1, -2):
        second = (twice * last[0] - back[0], twice * last[1] - back[1])
        first = (twice * second[0] - last[0], twice * second[1] - last[1])
        store(k, first, second)
        back, last = second, first


def offset_of(k):
    b, a = k >> 2, k & 3
    b3, a3 = (b >> 1) * (b & 1), (a >> 1) * (a & 1)
    dy = b + (b >> 1) - 2 * b3
    dz = a + 5 * (a >> 1) - 6 * a3 + 4 * a3 * (dy & 1)
    return dy, dz


def fold_row(j):
    return 8 * (j & 1) + 4 * (j >> 3 & 1) + 2 * (j >> 2 & 1) + (j >> 1 & 1)


def kernel(
    n_ray,
    n_pix,
    pos_hbm,
    dir_hbm,
    path_hbm,
    amp_hbm,
    grad_hbm,
    psf_hbm,
    out_hbm,
    pos_ref,
    dir_ref,
    path_ref,
    amp_ref,
    grad_ref,
    psf_ref,
    out_ref,
    pay,
    xt0,
    xt1,
    xt2,
    yt0,
    yt1,
    yt2,
    yf0,
    yf1,
    yf2,
    v_loc0,
    v_loc1,
    v_loc2,
    g2,
    v_rem,
    power,
    lhs,
    s_snd,
    s_rcv,
    tot,
    in_sem,
    out_sem,
    pay_send,
    pay_recv,
    g_sem,
    v_sem,
    s_send,
    s_recv,
    t_send,
    t_recv,
):
    me = lax.axis_index("ray")
    pix = lax.axis_index("pix")
    xt, yt, yf, v_loc = (xt0, xt1, xt2), (yt0, yt1, yt2), (yf0, yf1, yf2), (v_loc0, v_loc1, v_loc2)
    core = pix & 1
    pair = pix >> 1
    x_pos = pair & 3
    y_pos = me >> 2
    z_pos = 4 * (pair >> 2) + (me & 3)
    n_pair = n_pix // 2
    partner = pix + 1 - 2 * core
    rows = NPIX // n_pair
    cols = NPIX // n_ray
    half = pay.shape[2]
    count = 2 * half
    norm = 1.0 / math.sqrt(count * n_ray)

    def chip_at(dy, dz):
        y = (y_pos + dy) & 3
        z = (z_pos + dz) & 7
        return {"ray": 4 * y + (z & 3), "pix": 8 * (z >> 2) + (pix & 7)}

    def block_of(k):
        dy, dz = offset_of(k)
        return 4 * ((y_pos + dy) & 3) + ((z_pos + dz) & 3)

    loads = [
        pltpu.make_async_copy(src, dst, in_sem.at[i])
        for i, (src, dst) in enumerate(
            (
                (pos_hbm, pos_ref),
                (dir_hbm, dir_ref),
                (path_hbm, path_ref),
                (amp_hbm, amp_ref),
                (grad_hbm, grad_ref),
            )
        )
    ]
    for load in loads:
        load.start()

    def wait_bytes(ref, sem):
        pltpu.make_async_copy(ref, ref, sem).wait()

    barrier = pltpu.get_barrier_semaphore()

    def x_peer(dx, other):
        return {"pix": (pix & 8) + 2 * ((x_pos + dx) & 3) + (core + other - 2 * core * other)}

    x_others = [(dx, other) for dx in (2, 1, 3, 0) for other in range(2)][:7]
    x_others[6] = (0, 1)

    for dy, dz in [(dy, dz) for dy in range(4) for dz in (0, 1, 7, 2, 6)][1:]:
        pl.semaphore_signal(barrier, inc=1, device_id=chip_at(dy, dz), device_id_type=MESH)
    for dx, other in x_others:
        pl.semaphore_signal(barrier, inc=1, device_id=x_peer(dx, other), device_id_type=MESH)

    for load in loads[:4]:
        load.wait()
    mine = pl.ds(pl.multiple_of(core * half, 128), half)
    l_own = dir_ref[0:1, mine]
    m_own = dir_ref[1:2, mine]
    pay[me, 0:1, :] = (
        path_ref[0:1, mine] * (1.0 / two_pi) - l_own * pos_ref[0:1, mine] - m_own * pos_ref[1:2, mine]
    )
    pay[me, 1:2, :] = l_own
    pay[me, 2:3, :] = m_own
    pay[me, 3:4, :] = amp_ref[0:1, mine] * norm

    pl.semaphore_wait(barrier, 26)

    def pay_copy(k, slot):
        dy, dz = offset_of(k)
        return pltpu.make_async_remote_copy(
            src_ref=pay.at[me],
            dst_ref=pay.at[slot],
            send_sem=pay_send.at[0],
            recv_sem=pay_recv.at[slot],
            device_id=chip_at(4 - dy, 8 - dz),
            device_id_type=MESH,
        )

    for k in range(1, n_ray):
        pay_copy(k, me).start()

    loads[4].wait()
    line = lax.broadcasted_iota(jnp.int32, (rows // 2, rows // 2), 0)
    place = lax.broadcasted_iota(jnp.int32, (rows // 2, rows // 2), 1)
    flip = (line == core * place + (1 - core) * (rows // 2 - 1 - place)).astype(jnp.float32)

    def exact(left, right, dims):
        return lax.dot_general(
            left, right, dims, precision=lax.Precision.HIGHEST, preferred_element_type=jnp.float32
        )

    for wave in range(3):
        g2[core, wave] = exact(grad_ref[wave], flip, (((0,), (0,)), ((), ())))

    def g_copy(slot):
        return pltpu.make_async_remote_copy(
            src_ref=g2.at[core],
            dst_ref=g2.at[slot],
            send_sem=g_sem.at[0],
            recv_sem=g_sem.at[1],
            device_id={"pix": partner},
            device_id_type=MESH,
        )

    g_copy(core).start()

    row_start = pair * rows
    col_start = me * cols
    sub = lax.broadcasted_iota(jnp.int32, (8, half), 0)
    x_mid = (row_start + rows // 2).astype(jnp.float32) - 0.5 * NPIX
    y_mid = (col_start + cols // 2).astype(jnp.float32) - 0.5 * NPIX
    x_base = sub.astype(jnp.float32) + (0.25 * rows + 0.5)
    y_base = sub.astype(jnp.float32) + (y_mid + 0.5)
    wave_of = lax.rem(sub, 3)
    step_scale = 8.0 * jnp.where(
        wave_of == 0, wave_scales[0], jnp.where(wave_of == 1, wave_scales[1], wave_scales[2])
    )

    for wave in range(3):
        v_loc[wave][...] = jnp.zeros_like(v_loc[wave])

    def tables(block):
        rho = jnp.broadcast_to(pay[block, 0:1, :], (8, half))
        l_all = jnp.broadcast_to(pay[block, 1:2, :], (8, half))
        m_all = jnp.broadcast_to(pay[block, 2:3, :], (8, half))
        amp = jnp.broadcast_to(pay[block, 3:4, :], (8, half))
        step_c, step_s = cos_sin_turns(step_scale * jnp.where(sub < 3, l_all, m_all))
        x_turns = l_all * x_base
        y_turns = (rho + l_all * x_mid) + m_all * y_base

        def row_of(table, index):
            return jnp.broadcast_to(table[index : index + 1, :], (8, half))

        def one_wave(wave):
            scale = wave_scales[wave]

            def store_x(k, first, second):
                for part in range(2):
                    tile = jnp.concatenate([first[part], second[part]], axis=0)
                    at = part * (rows // 2) + 8 * k
                    xt[wave][block, at : at + 16, :] = tile.astype(jnp.bfloat16)

            def store_y(k, first, second):
                for part in range(2):
                    tile = jnp.concatenate([first[part], second[part]], axis=0)
                    at = part * cols + 8 * k
                    yf[wave][block, at : at + 16, :] = tile
                    yt[wave][block, at : at + 16, :] = tile.astype(jnp.bfloat16)

            ladder(
                cos_sin_turns(scale * x_turns),
                row_of(step_c, wave),
                row_of(step_s, wave),
                rows // 16,
                store_x,
            )
            bc, bs = cos_sin_turns(scale * y_turns)
            ladder(
                (amp * bc, amp * bs),
                row_of(step_c, wave + 3),
                row_of(step_s, wave + 3),
                cols // 8,
                store_y,
            )

        return one_wave

    def gather_field(block, wave, keep):
        total = v_loc[wave][...] + lax.dot_general(
            yt[wave][block],
            xt[wave][block],
            (((1,), (1,)), ((), ())),
            preferred_element_type=jnp.float32,
        )
        v_loc[wave][...] = jnp.where(keep, total, 0.0)

    def forward_step(k, carry):
        before = block_of((k - 1) & (n_ray - 1))
        block = block_of(k)

        @pl.when(k > 0)
        def _():
            pay_copy(k, block).wait_recv()

        make = tables(block)
        for wave in range(3):
            gather_field(before, wave, k > 0)
        for wave in range(3):
            make(wave)
        return carry

    lax.fori_loop(0, n_ray, forward_step, 0)
    v_copies = [
        pltpu.make_async_remote_copy(
            src_ref=v_loc[wave],
            dst_ref=v_rem.at[wave],
            send_sem=v_sem.at[0, wave],
            recv_sem=v_sem.at[1, wave],
            device_id={"pix": partner},
            device_id_type=MESH,
        )
        for wave in range(3)
    ]
    for wave in range(3):
        gather_field(block_of(n_ray - 1), wave, True)
        v_copies[wave].start()
    g_copy(1 - core).wait_recv()

    low = lax.broadcasted_iota(jnp.int32, (cols, rows), 1) < rows // 2
    distance = (lax.broadcasted_iota(jnp.int32, (cols, rows), 1) & (rows // 2 - 1)).astype(
        jnp.float32
    ) + 0.5

    def swap(a):
        return pltpu.roll(a, rows // 2, 1)

    for wave in range(3):
        v_copies[wave].wait_recv()
        top = v_loc[wave][0:cols, :] + v_rem[wave, 0:cols, :]
        bot = v_loc[wave][cols:, :] + v_rem[wave, cols:, :]
        top_s, bot_s = swap(top), swap(bot)
        u_re = jnp.where(low, top - bot_s, top_s + bot)
        u_im = jnp.where(low, bot + top_s, bot_s - top)
        power[wave] = u_re * u_re + u_im * u_im
        weight = 2.0 * jnp.concatenate([g2[1, wave], g2[0, wave]], axis=1)
        g_re, g_im = weight * u_re, weight * u_im
        r_re, r_im = swap(g_re), swap(g_im)
        plus_re, less_re = g_re + r_re, g_re - r_re
        plus_im, less_im = g_im + r_im, g_im - r_im
        for i, table in enumerate(
            (
                jnp.where(low, plus_re, -less_im),
                jnp.where(low, plus_im, less_re),
                jnp.where(low, less_re, plus_im) * distance,
                jnp.where(low, less_im, -plus_re) * distance,
            )
        ):
            lhs[wave, i * cols : (i + 1) * cols, :] = table.astype(jnp.bfloat16)

    here = 8 * y_pos + z_pos

    def s_copy(k, far):
        dy, dz = offset_of(k)
        return pltpu.make_async_remote_copy(
            src_ref=s_snd.at[k],
            dst_ref=s_rcv.at[here],
            send_sem=s_send.at[0],
            recv_sem=s_recv.at[0],
            device_id=chip_at(dy, dz + 4 * far),
            device_id_type=MESH,
        )

    def project(block, wave):
        return lax.dot_general(
            lhs[wave],
            xt[wave][block],
            (((1,), (0,)), ((), ())),
            preferred_element_type=jnp.float32,
        )

    sub_f = sub.astype(jnp.float32)

    def contract(block, wave, sums):
        d_wave = project(block, wave)
        s1, s2, s3, s4 = sums
        zi = zx = zy = None
        for t in range(cols // 8):
            at = 8 * t
            br = yf[wave][block, at : at + 8, :]
            bi = yf[wave][block, cols + at : cols + at + 8, :]
            dbr = d_wave[at : at + 8, :]
            dbi = d_wave[cols + at : cols + at + 8, :]
            dxr = d_wave[2 * cols + at : 2 * cols + at + 8, :]
            dxi = d_wave[3 * cols + at : 3 * cols + at + 8, :]
            d = br * dbi - bi * dbr
            dx = br * dxi - bi * dxr
            dy = d * (sub_f + (at - 0.5 * cols + 0.5))
            s4 = s4 + (br * dbr + bi * dbi)
            zi, zx, zy = (d, dx, dy) if t == 0 else (zi + d, zx + dx, zy + dy)
        scale = wave_scales[wave]
        s1 = s1 + scale * zi
        s2 = s2 + (scale * two_pi) * (x_mid * zi + zx)
        s3 = s3 + (scale * two_pi) * (y_mid * zi + zy)
        return s1, s2, s3, s4

    def order(i):
        a = (i >> 2) & 3
        return 4 * ((3 + ((4 - a) >> 2) - (i & 3)) & 3) + a

    def fold(tiles):
        lane_row = lax.broadcasted_iota(jnp.int32, (8, 128), 0)
        for shift in (4, 2, 1):
            keep = (lane_row & shift) == 0
            n = len(tiles) // 2
            tiles = [
                jnp.where(keep, a + pltpu.roll(a, 8 - shift, 0), b + pltpu.roll(b, shift, 0))
                for a, b in zip(tiles[:n], tiles[n:])
            ]
        return jnp.concatenate(tiles, axis=0)

    def one_block(k, block):
        sums = (jnp.zeros((8, half), jnp.float32),) * 4
        for wave in range(3):
            sums = contract(block, wave, sums)
        tiles = [s[:, 128 * t : 128 * t + 128] for s in sums for t in range(half // 128)]
        s_snd[k] = fold(tiles).astype(jnp.bfloat16)

    def backward_step(i, carry):
        ks = [order(2 * i + n) for n in range(2)]
        for k in ks:
            one_block(k, block_of(k))
        for k in ks:
            s_copy(k, 1).start()

        @pl.when(i > 0)
        def _():
            s_copy(ks[0], 0).start()

        s_copy(ks[1], 0).start()
        return carry

    lax.fori_loop(0, n_ray // 2, backward_step, 0)
    s_rcv[here] = s_snd[0]
    wait_bytes(s_rcv.at[0:31], s_recv.at[0])
    total = s_rcv[0].astype(jnp.float32)
    for b in range(1, 32):
        total = total + s_rcv[b].astype(jnp.float32)
    tot[4 * core + x_pos] = total

    for dx, other in x_others:
        pltpu.make_async_remote_copy(
            src_ref=tot.at[4 * core + x_pos],
            dst_ref=tot.at[4 * core + x_pos],
            send_sem=t_send.at[0],
            recv_sem=t_recv.at[0],
            device_id=x_peer(dx, other),
            device_id_type=MESH,
        ).start()
    for wave in range(3):
        above, below = power[wave, :, : rows // 2], power[wave, :, rows // 2 :]
        psf_ref[wave] = exact(flip, jnp.where(core == 1, above, below), (((1,), (1,)), ((), ())))
    psf_store = pltpu.make_async_copy(psf_ref, psf_hbm, out_sem.at[0])
    psf_store.start()
    wait_bytes(tot.at[0:7], t_recv.at[0])
    tiles = half // 128
    for h in range(2):
        total = tot[4 * h]
        for b in range(1, 4):
            total = total + tot[4 * h + b]
        for t in range(tiles):
            at = slice(h * half + 128 * t, h * half + 128 * t + 128)
            s1, s2, s3, s4 = (total[r : r + 1] for r in (fold_row(tiles * i + t) for i in range(4)))
            out_ref[0:1, at] = s1
            out_ref[1:2, at] = -two_pi * dir_ref[0:1, at] * s1
            out_ref[2:3, at] = -two_pi * dir_ref[1:2, at] * s1
            out_ref[3:4, at] = (s2 - two_pi * pos_ref[0:1, at] * s1) * (1.0 / NPIX)
            out_ref[4:5, at] = (s3 - two_pi * pos_ref[1:2, at] * s1) * (1.0 / NPIX)
            out_ref[5:6, at] = s4 / amp_ref[0:1, at]
    out_store = pltpu.make_async_copy(out_ref, out_hbm, out_sem.at[1])
    out_store.start()

    wait_bytes(pay.at[0 : n_ray - 1], pay_send.at[0])
    wait_bytes(s_rcv.at[0:31], s_send.at[0])
    wait_bytes(tot.at[0:7], t_send.at[0])
    g_copy(core).wait_send()
    for v_copy in v_copies:
        v_copy.wait_send()
    psf_store.wait()
    out_store.wait()


def on_device(n_ray, n_pix, positions, directions, path, amplitude, psf_grad):
    count = positions.shape[1]
    half = count // 2
    n_pair = n_pix // 2
    rows = NPIX // n_pair
    cols = NPIX // n_ray
    f32 = jnp.float32
    bf16 = jnp.bfloat16
    hbm_space = pl.BlockSpec(memory_space=pltpu.HBM)
    any_space = pl.BlockSpec(memory_space=pl.ANY)
    dma = pltpu.SemaphoreType.DMA
    return pl.pallas_call(
        functools.partial(kernel, n_ray, n_pix),
        out_shape=(
            jax.ShapeDtypeStruct(psf_grad.shape, f32),
            jax.ShapeDtypeStruct((6, count), f32),
        ),
        in_specs=[hbm_space] * 5,
        out_specs=(any_space, any_space),
        scratch_shapes=[
            pltpu.VMEM((2, count), f32),
            pltpu.VMEM((2, count), f32),
            pltpu.VMEM((1, count), f32),
            pltpu.VMEM((1, count), f32),
            pltpu.VMEM(psf_grad.shape, f32),
            pltpu.VMEM(psf_grad.shape, f32),
            pltpu.VMEM((6, count), f32),
            pltpu.VMEM((n_ray, 4, half), f32),
            *[pltpu.VMEM((n_ray, rows, half), bf16)] * 3,
            *[pltpu.VMEM((n_ray, 2 * cols, half), bf16)] * 3,
            *[pltpu.VMEM((n_ray, 2 * cols, half), f32)] * 3,
            *[pltpu.VMEM((2 * cols, rows), f32)] * 3,
            pltpu.VMEM((2, 3, cols, rows // 2), f32),
            pltpu.VMEM((3, 2 * cols, rows), f32),
            pltpu.VMEM((3, cols, rows), f32),
            pltpu.VMEM((3, 4 * cols, rows), bf16),
            pltpu.VMEM((n_ray, half // 32, 128), bf16),
            pltpu.VMEM((32, half // 32, 128), bf16),
            pltpu.VMEM((8, half // 32, 128), f32),
            dma((5,)),
            dma((2,)),
            dma((1,)),
            dma((n_ray,)),
            dma((2,)),
            dma((2, 3)),
            dma((1,)),
            dma((1,)),
            dma((1,)),
            dma((1,)),
        ],
        compiler_params=pltpu.CompilerParams(
            collective_id=0, has_side_effects=True, vmem_limit_bytes=48 * 1024 * 1024
        ),
        name="ray_wave",
    )(*[
        pltpu.with_memory_space_constraint(v, pltpu.HBM)
        for v in (positions, directions, path.reshape(1, count), amplitude.reshape(1, count), psf_grad)
    ])


def solution(mesh):
    in_specs = (P(None, "ray"), P(None, "ray"), P("ray"), P("ray"), P(None, "pix", "ray"))
    out_specs = (P(None, "pix", "ray"), P(None, "ray"))
    body = functools.partial(on_device, mesh.shape["ray"], mesh.shape["pix"])
    return jax.shard_map(
        body, mesh=mesh, in_specs=in_specs, out_specs=out_specs, check_vma=False
    )
```

```python
import functools
import math

import jax
import jax.numpy as jnp
from jax import lax
from jax.experimental import pallas as pl
from jax.experimental.pallas import tpu as pltpu
from jax.sharding import PartitionSpec as P

NPIX = 1024

wave_scales = (1.2088, 1.0, 0.8953)
two_pi = 2.0 * math.pi
MESH = pl.DeviceIdType.MESH

COS_COEF = (
    0.9999999890590201,
    -19.739204499453688,
    64.93911745988827,
    -85.45013953077586,
    60.16763095018129,
    -25.96759924584206,
    6.528658157862129,
)
SIN_COEF = (
    6.283185302511498,
    -41.341700405316736,
    81.60513138576982,
    -76.70301535347629,
    42.02592698341473,
    -14.899846660399582,
    3.2381375010236435,
)


def horner(coef, z):
    total = coef[-1] * z + coef[-2]
    for c in coef[-3::-1]:
        total = total * z + c
    return total


def cos_sin_turns(turns):
    frac = turns - jnp.round(turns)
    z = frac * frac
    return horner(COS_COEF, z), horner(SIN_COEF, z) * frac


def ladder(base, step_c, step_s, ntiles, store):
    c0, s0 = base
    cc, ss, cs, sc = c0 * step_c, s0 * step_s, c0 * step_s, s0 * step_c
    twice = step_c + step_c
    up = (cc - ss, sc + cs)
    down = (cc + ss, sc - cs)
    mid = ntiles // 2
    store(mid, base, up)
    back, last = base, up
    for k in range(mid + 2, ntiles, 2):
        first = (twice * last[0] - back[0], twice * last[1] - back[1])
        second = (twice * first[0] - last[0], twice * first[1] - last[1])
        store(k, first, second)
        back, last = first, second
    back, last = base, down
    nxt = (twice * last[0] - back[0], twice * last[1] - back[1])
    store(mid - 2, nxt, last)
    back, last = last, nxt
    for k in range(mid - 4, -1, -2):
        second = (twice * last[0] - back[0], twice * last[1] - back[1])
        first = (twice * second[0] - last[0], twice * second[1] - last[1])
        store(k, first, second)
        back, last = second, first


def offset_of(k):
    b, a = k >> 2, k & 3
    b3, a3 = (b >> 1) * (b & 1), (a >> 1) * (a & 1)
    dy = b + (b >> 1) - 2 * b3
    dz = a + 5 * (a >> 1) - 6 * a3 + 4 * a3 * (dy & 1)
    return dy, dz


def fold_row(j):
    return 8 * (j & 1) + 4 * (j >> 3 & 1) + 2 * (j >> 2 & 1) + (j >> 1 & 1)


def kernel(
    n_ray,
    n_pix,
    pos_hbm,
    dir_hbm,
    path_hbm,
    amp_hbm,
    grad_hbm,
    psf_hbm,
    out_hbm,
    pos_ref,
    dir_ref,
    path_ref,
    amp_ref,
    grad_ref,
    psf_ref,
    out_ref,
    pay,
    xt0,
    xt1,
    xt2,
    yt0,
    yt1,
    yt2,
    yf0,
    yf1,
    yf2,
    v_loc0,
    v_loc1,
    v_loc2,
    g2,
    v_rem,
    power,
    lhs,
    s_snd,
    s_rcv,
    tot,
    in_sem,
    out_sem,
    pay_send,
    pay_recv,
    g_sem,
    v_sem,
    s_send,
    s_recv,
    t_send,
    t_recv,
):
    me = lax.axis_index("ray")
    pix = lax.axis_index("pix")
    xt, yt, yf, v_loc = (xt0, xt1, xt2), (yt0, yt1, yt2), (yf0, yf1, yf2), (v_loc0, v_loc1, v_loc2)
    core = pix & 1
    pair = pix >> 1
    x_pos = pair & 3
    y_pos = me >> 2
    z_pos = 4 * (pair >> 2) + (me & 3)
    n_pair = n_pix // 2
    partner = pix + 1 - 2 * core
    rows = NPIX // n_pair
    cols = NPIX // n_ray
    half = pay.shape[2]
    count = 2 * half
    norm = 1.0 / math.sqrt(count * n_ray)

    def chip_at(dy, dz):
        y = (y_pos + dy) & 3
        z = (z_pos + dz) & 7
        return {"ray": 4 * y + (z & 3), "pix": 8 * (z >> 2) + (pix & 7)}

    def block_of(k):
        dy, dz = offset_of(k)
        return 4 * ((y_pos + dy) & 3) + ((z_pos + dz) & 3)

    loads = [
        pltpu.make_async_copy(src, dst, in_sem.at[i])
        for i, (src, dst) in enumerate(
            (
                (pos_hbm, pos_ref),
                (dir_hbm, dir_ref),
                (path_hbm, path_ref),
                (amp_hbm, amp_ref),
                (grad_hbm, grad_ref),
            )
        )
    ]
    for load in loads:
        load.start()

    def wait_bytes(ref, sem):
        pltpu.make_async_copy(ref, ref, sem).wait()

    barrier = pltpu.get_barrier_semaphore()

    def x_peer(dx, other):
        return {"pix": (pix & 8) + 2 * ((x_pos + dx) & 3) + (core + other - 2 * core * other)}

    x_others = [(dx, other) for dx in (2, 1, 3, 0) for other in range(2)][:7]
    x_others[6] = (0, 1)

    for dy, dz in ((2, 2), (2, 6), (1, 2), (1, 6), (2, 1), (2, 7), (3, 2), (3, 6), (0, 2), (0, 6), (1, 1), (1, 7), (2, 0), (3, 1), (3, 7), (0, 1), (0, 7), (1, 0), (3, 0)):
        pl.semaphore_signal(barrier, inc=1, device_id=chip_at(dy, dz), device_id_type=MESH)
    for dx, other in x_others:
        pl.semaphore_signal(barrier, inc=1, device_id=x_peer(dx, other), device_id_type=MESH)

    for load in loads[:4]:
        load.wait()
    mine = pl.ds(pl.multiple_of(core * half, 128), half)
    l_own = dir_ref[0:1, mine]
    m_own = dir_ref[1:2, mine]
    pay[me, 0:1, :] = (
        path_ref[0:1, mine] * (1.0 / two_pi) - l_own * pos_ref[0:1, mine] - m_own * pos_ref[1:2, mine]
    )
    pay[me, 1:2, :] = l_own
    pay[me, 2:3, :] = m_own
    pay[me, 3:4, :] = amp_ref[0:1, mine] * norm

    pl.semaphore_wait(barrier, 26)

    def pay_copy(k, slot):
        dy, dz = offset_of(k)
        return pltpu.make_async_remote_copy(
            src_ref=pay.at[me],
            dst_ref=pay.at[slot],
            send_sem=pay_send.at[0],
            recv_sem=pay_recv.at[slot],
            device_id=chip_at(4 - dy, 8 - dz),
            device_id_type=MESH,
        )

    for k in range(1, n_ray):
        pay_copy(k, me).start()

    loads[4].wait()
    line = lax.broadcasted_iota(jnp.int32, (rows // 2, rows // 2), 0)
    place = lax.broadcasted_iota(jnp.int32, (rows // 2, rows // 2), 1)
    flip = (line == core * place + (1 - core) * (rows // 2 - 1 - place)).astype(jnp.float32)

    def exact(left, right, dims):
        return lax.dot_general(
            left, right, dims, precision=lax.Precision.HIGHEST, preferred_element_type=jnp.float32
        )

    for wave in range(3):
        g2[core, wave] = exact(grad_ref[wave], flip, (((0,), (0,)), ((), ())))

    def g_copy(slot):
        return pltpu.make_async_remote_copy(
            src_ref=g2.at[core],
            dst_ref=g2.at[slot],
            send_sem=g_sem.at[0],
            recv_sem=g_sem.at[1],
            device_id={"pix": partner},
            device_id_type=MESH,
        )

    g_copy(core).start()

    row_start = pair * rows
    col_start = me * cols
    sub = lax.broadcasted_iota(jnp.int32, (8, half), 0)
    x_mid = (row_start + rows // 2).astype(jnp.float32) - 0.5 * NPIX
    y_mid = (col_start + cols // 2).astype(jnp.float32) - 0.5 * NPIX
    x_base = sub.astype(jnp.float32) + (0.25 * rows + 0.5)
    y_base = sub.astype(jnp.float32) + (y_mid + 0.5)
    wave_of = lax.rem(sub, 3)
    step_scale = 8.0 * jnp.where(
        wave_of == 0, wave_scales[0], jnp.where(wave_of == 1, wave_scales[1], wave_scales[2])
    )

    for wave in range(3):
        v_loc[wave][...] = jnp.zeros_like(v_loc[wave])

    def tables(block):
        rho = jnp.broadcast_to(pay[block, 0:1, :], (8, half))
        l_all = jnp.broadcast_to(pay[block, 1:2, :], (8, half))
        m_all = jnp.broadcast_to(pay[block, 2:3, :], (8, half))
        amp = jnp.broadcast_to(pay[block, 3:4, :], (8, half))
        step_c, step_s = cos_sin_turns(step_scale * jnp.where(sub < 3, l_all, m_all))
        x_turns = l_all * x_base
        y_turns = (rho + l_all * x_mid) + m_all * y_base

        def row_of(table, index):
            return jnp.broadcast_to(table[index : index + 1, :], (8, half))

        def one_wave(wave):
            scale = wave_scales[wave]

            def store_x(k, first, second):
                for part in range(2):
                    tile = jnp.concatenate([first[part], second[part]], axis=0)
                    at = part * (rows // 2) + 8 * k
                    xt[wave][block, at : at + 16, :] = tile.astype(jnp.bfloat16)

            def store_y(k, first, second):
                for part in range(2):
                    tile = jnp.concatenate([first[part], second[part]], axis=0)
                    at = part * cols + 8 * k
                    yf[wave][block, at : at + 16, :] = tile
                    yt[wave][block, at : at + 16, :] = tile.astype(jnp.bfloat16)

            ladder(
                cos_sin_turns(scale * x_turns),
                row_of(step_c, wave),
                row_of(step_s, wave),
                rows // 16,
                store_x,
            )
            bc, bs = cos_sin_turns(scale * y_turns)
            ladder(
                (amp * bc, amp * bs),
                row_of(step_c, wave + 3),
                row_of(step_s, wave + 3),
                cols // 8,
                store_y,
            )

        return one_wave

    def gather_field(block, wave, keep):
        total = v_loc[wave][...] + lax.dot_general(
            yt[wave][block],
            xt[wave][block],
            (((1,), (1,)), ((), ())),
            preferred_element_type=jnp.float32,
        )
        v_loc[wave][...] = jnp.where(keep, total, 0.0)

    def forward_step(k, carry):
        before = block_of((k - 1) & (n_ray - 1))
        block = block_of(k)

        @pl.when(k > 0)
        def _():
            pay_copy(k, block).wait_recv()

        make = tables(block)
        for wave in range(3):
            gather_field(before, wave, k > 0)
        for wave in range(3):
            make(wave)
        return carry

    lax.fori_loop(0, n_ray, forward_step, 0)
    v_copies = [
        pltpu.make_async_remote_copy(
            src_ref=v_loc[wave],
            dst_ref=v_rem.at[wave],
            send_sem=v_sem.at[0, wave],
            recv_sem=v_sem.at[1, wave],
            device_id={"pix": partner},
            device_id_type=MESH,
        )
        for wave in range(3)
    ]
    for wave in range(3):
        gather_field(block_of(n_ray - 1), wave, True)
        v_copies[wave].start()
    g_copy(1 - core).wait_recv()

    low = lax.broadcasted_iota(jnp.int32, (cols, rows), 1) < rows // 2
    distance = (lax.broadcasted_iota(jnp.int32, (cols, rows), 1) & (rows // 2 - 1)).astype(
        jnp.float32
    ) + 0.5

    def swap(a):
        return pltpu.roll(a, rows // 2, 1)

    for wave in range(3):
        v_copies[wave].wait_recv()
        top = v_loc[wave][0:cols, :] + v_rem[wave, 0:cols, :]
        bot = v_loc[wave][cols:, :] + v_rem[wave, cols:, :]
        top_s, bot_s = swap(top), swap(bot)
        u_re = jnp.where(low, top - bot_s, top_s + bot)
        u_im = jnp.where(low, bot + top_s, bot_s - top)
        power[wave] = u_re * u_re + u_im * u_im
        weight = 2.0 * jnp.concatenate([g2[1, wave], g2[0, wave]], axis=1)
        g_re, g_im = weight * u_re, weight * u_im
        r_re, r_im = swap(g_re), swap(g_im)
        plus_re, less_re = g_re + r_re, g_re - r_re
        plus_im, less_im = g_im + r_im, g_im - r_im
        for i, table in enumerate(
            (
                jnp.where(low, plus_re, -less_im),
                jnp.where(low, plus_im, less_re),
                jnp.where(low, less_re, plus_im) * distance,
                jnp.where(low, less_im, -plus_re) * distance,
            )
        ):
            lhs[wave, i * cols : (i + 1) * cols, :] = table.astype(jnp.bfloat16)

    here = 8 * y_pos + z_pos

    def s_copy(k, far):
        dy, dz = offset_of(k)
        return pltpu.make_async_remote_copy(
            src_ref=s_snd.at[k],
            dst_ref=s_rcv.at[here],
            send_sem=s_send.at[0],
            recv_sem=s_recv.at[0],
            device_id=chip_at(dy, dz + 4 * far),
            device_id_type=MESH,
        )

    def project(block, wave):
        return lax.dot_general(
            lhs[wave],
            xt[wave][block],
            (((1,), (0,)), ((), ())),
            preferred_element_type=jnp.float32,
        )

    sub_f = sub.astype(jnp.float32)

    def contract(block, wave, sums):
        d_wave = project(block, wave)
        s1, s2, s3, s4 = sums
        zi = zx = zy = None
        for t in range(cols // 8):
            at = 8 * t
            br = yf[wave][block, at : at + 8, :]
            bi = yf[wave][block, cols + at : cols + at + 8, :]
            dbr = d_wave[at : at + 8, :]
            dbi = d_wave[cols + at : cols + at + 8, :]
            dxr = d_wave[2 * cols + at : 2 * cols + at + 8, :]
            dxi = d_wave[3 * cols + at : 3 * cols + at + 8, :]
            d = br * dbi - bi * dbr
            dx = br * dxi - bi * dxr
            dy = d * (sub_f + (at - 0.5 * cols + 0.5))
            s4 = s4 + (br * dbr + bi * dbi)
            zi, zx, zy = (d, dx, dy) if t == 0 else (zi + d, zx + dx, zy + dy)
        scale = wave_scales[wave]
        s1 = s1 + scale * zi
        s2 = s2 + (scale * two_pi) * (x_mid * zi + zx)
        s3 = s3 + (scale * two_pi) * (y_mid * zi + zy)
        return s1, s2, s3, s4

    def order(i):
        a = (i >> 2) & 3
        return 4 * ((3 + ((4 - a) >> 2) - (i & 3)) & 3) + a

    def fold(tiles):
        lane_row = lax.broadcasted_iota(jnp.int32, (8, 128), 0)
        for shift in (4, 2, 1):
            keep = (lane_row & shift) == 0
            n = len(tiles) // 2
            tiles = [
                jnp.where(keep, a + pltpu.roll(a, 8 - shift, 0), b + pltpu.roll(b, shift, 0))
                for a, b in zip(tiles[:n], tiles[n:])
            ]
        return jnp.concatenate(tiles, axis=0)

    def one_block(k, block):
        sums = (jnp.zeros((8, half), jnp.float32),) * 4
        for wave in range(3):
            sums = contract(block, wave, sums)
        tiles = [s[:, 128 * t : 128 * t + 128] for s in sums for t in range(half // 128)]
        s_snd[k] = fold(tiles).astype(jnp.bfloat16)

    def backward_step(i, carry):
        ks = [order(2 * i + n) for n in range(2)]
        for k in ks:
            one_block(k, block_of(k))
        for k in ks:
            s_copy(k, 1).start()

        @pl.when(i > 0)
        def _():
            s_copy(ks[0], 0).start()

        s_copy(ks[1], 0).start()
        return carry

    lax.fori_loop(0, n_ray // 2, backward_step, 0)
    s_rcv[here] = s_snd[0]
    wait_bytes(s_rcv.at[0:31], s_recv.at[0])
    total = s_rcv[0].astype(jnp.float32)
    for b in range(1, 32):
        total = total + s_rcv[b].astype(jnp.float32)
    tot[4 * core + x_pos] = total

    for dx, other in x_others:
        pltpu.make_async_remote_copy(
            src_ref=tot.at[4 * core + x_pos],
            dst_ref=tot.at[4 * core + x_pos],
            send_sem=t_send.at[0],
            recv_sem=t_recv.at[0],
            device_id=x_peer(dx, other),
            device_id_type=MESH,
        ).start()
    for wave in range(3):
        above, below = power[wave, :, : rows // 2], power[wave, :, rows // 2 :]
        psf_ref[wave] = exact(flip, jnp.where(core == 1, above, below), (((1,), (1,)), ((), ())))
    psf_store = pltpu.make_async_copy(psf_ref, psf_hbm, out_sem.at[0])
    psf_store.start()
    wait_bytes(tot.at[0:7], t_recv.at[0])
    tiles = half // 128
    for h in range(2):
        total = tot[4 * h]
        for b in range(1, 4):
            total = total + tot[4 * h + b]
        for t in range(tiles):
            at = slice(h * half + 128 * t, h * half + 128 * t + 128)
            s1, s2, s3, s4 = (total[r : r + 1] for r in (fold_row(tiles * i + t) for i in range(4)))
            out_ref[0:1, at] = s1
            out_ref[1:2, at] = -two_pi * dir_ref[0:1, at] * s1
            out_ref[2:3, at] = -two_pi * dir_ref[1:2, at] * s1
            out_ref[3:4, at] = (s2 - two_pi * pos_ref[0:1, at] * s1) * (1.0 / NPIX)
            out_ref[4:5, at] = (s3 - two_pi * pos_ref[1:2, at] * s1) * (1.0 / NPIX)
            out_ref[5:6, at] = s4 / amp_ref[0:1, at]
    out_store = pltpu.make_async_copy(out_ref, out_hbm, out_sem.at[1])
    out_store.start()

    wait_bytes(pay.at[0 : n_ray - 1], pay_send.at[0])
    wait_bytes(s_rcv.at[0:31], s_send.at[0])
    wait_bytes(tot.at[0:7], t_send.at[0])
    g_copy(core).wait_send()
    for v_copy in v_copies:
        v_copy.wait_send()
    psf_store.wait()
    out_store.wait()


def on_device(n_ray, n_pix, positions, directions, path, amplitude, psf_grad):
    count = positions.shape[1]
    half = count // 2
    n_pair = n_pix // 2
    rows = NPIX // n_pair
    cols = NPIX // n_ray
    f32 = jnp.float32
    bf16 = jnp.bfloat16
    hbm_space = pl.BlockSpec(memory_space=pltpu.HBM)
    any_space = pl.BlockSpec(memory_space=pl.ANY)
    dma = pltpu.SemaphoreType.DMA
    return pl.pallas_call(
        functools.partial(kernel, n_ray, n_pix),
        out_shape=(
            jax.ShapeDtypeStruct(psf_grad.shape, f32),
            jax.ShapeDtypeStruct((6, count), f32),
        ),
        in_specs=[hbm_space] * 5,
        out_specs=(any_space, any_space),
        scratch_shapes=[
            pltpu.VMEM((2, count), f32),
            pltpu.VMEM((2, count), f32),
            pltpu.VMEM((1, count), f32),
            pltpu.VMEM((1, count), f32),
            pltpu.VMEM(psf_grad.shape, f32),
            pltpu.VMEM(psf_grad.shape, f32),
            pltpu.VMEM((6, count), f32),
            pltpu.VMEM((n_ray, 4, half), f32),
            *[pltpu.VMEM((n_ray, rows, half), bf16)] * 3,
            *[pltpu.VMEM((n_ray, 2 * cols, half), bf16)] * 3,
            *[pltpu.VMEM((n_ray, 2 * cols, half), f32)] * 3,
            *[pltpu.VMEM((2 * cols, rows), f32)] * 3,
            pltpu.VMEM((2, 3, cols, rows // 2), f32),
            pltpu.VMEM((3, 2 * cols, rows), f32),
            pltpu.VMEM((3, cols, rows), f32),
            pltpu.VMEM((3, 4 * cols, rows), bf16),
            pltpu.VMEM((n_ray, half // 32, 128), bf16),
            pltpu.VMEM((32, half // 32, 128), bf16),
            pltpu.VMEM((8, half // 32, 128), f32),
            dma((5,)),
            dma((2,)),
            dma((1,)),
            dma((n_ray,)),
            dma((2,)),
            dma((2, 3)),
            dma((1,)),
            dma((1,)),
            dma((1,)),
            dma((1,)),
        ],
        compiler_params=pltpu.CompilerParams(
            collective_id=0, has_side_effects=True, vmem_limit_bytes=48 * 1024 * 1024
        ),
        name="ray_wave",
    )(*[
        pltpu.with_memory_space_constraint(v, pltpu.HBM)
        for v in (positions, directions, path.reshape(1, count), amplitude.reshape(1, count), psf_grad)
    ])


def solution(mesh):
    in_specs = (P(None, "ray"), P(None, "ray"), P("ray"), P("ray"), P(None, "pix", "ray"))
    out_specs = (P(None, "pix", "ray"), P(None, "ray"))
    body = functools.partial(on_device, mesh.shape["ray"], mesh.shape["pix"])
    return jax.shard_map(
        body, mesh=mesh, in_specs=in_specs, out_specs=out_specs, check_vma=False
    )
```
